32 devices in a mesh: group: 2 (over x), tile: 16 (over z, y, core).
Axes of the slice: x: 2, y: 2, z: 4, core: 2. Of those that a mesh axis runs over, the one named last changes fastest.
Arguments:
- latents: bfloat16 [384, 16, 128], P(('group', 'tile')), parts along dimension 0, may hold values from -6 to 6
- clip_index: int32 [8], P('group'), parts along dimension 0, may hold values from 0 to 1, never falling along the last dimension, each value on 1 to 3 neighbouring positions
- first_conv: bfloat16 [3, 3, 3, 16, 384], replicated, may hold values from -0.3125 to 0.3125
- first_gain: float32 [384], replicated, may hold values from 0.4 to 1.6
- middle_conv: bfloat16 [3, 3, 3, 384, 384], replicated, may hold values from -0.0625 to 0.0625
- head_gain: float32 [384], replicated, may hold values from 0.4 to 1.6
- head_weight: bfloat16 [384, 48], replicated, may hold values from -0.3125 to 0.3125
Outputs:
- pixels: float32 [32, 2, 3, 48, 128], P(('group', 'tile')), parts along dimension 0
The draws below stay inside these ranges and needn't reach their ends.
There are 2 independent parts, one for each index of `group`. The reference program is written for one: setup_inputs(seed, part) draws one part's arguments, and reference() takes and returns one part's arrays. A program takes and returns all parts, laid end to end along the dimension named above; an argument that names none is the same for every part. Nothing has to cross between parts.
Inputs may be any that keep to these rules, and one draw needn't show every extreme that they name: `clip_index`: clip numbers never fall along the frames; each clip holds 1 to 3 consecutive frames.
All inputs are finite; a program needn't handle non-finite values.
Results may differ from the reference program's by a relative error of at most 0.01.
Values may be sent and summed in bfloat16 or wider, within the bound.
A program may use at most 128 MiB of HBM per device.

```python
import math
import jax
import jax.numpy as jnp
import numpy as np
from jax import lax

CLAT = 16
CH = 384
PATCH = 16
STRIPS = 8
TF = 2
WS = 16
HL = 48
BLOCKS = 2
TILES = 16
FRAMES = 4
WL = 128
CLIPS = 2
CLIP_MOST = 3


def block_levels(rng, extent, pieces, smallest, top_value):
    def one(axis_at, shards_of):
        draws = jax.random.uniform(jax.random.fold_in(jax.random.fold_in(rng, 6), axis_at), (shards_of,), jnp.float32, smallest / len(pieces), top_value / len(pieces))
        return jnp.repeat(jnp.exp(draws), extent[axis_at] // shards_of).reshape((-1,) + (1,) * (len(extent) - axis_at - 1))

    loudness = one(*pieces[0])
    for cut in pieces[1:]:
        loudness = loudness * one(*cut)
    return loudness


def profile(count, total, most, slope):
    portions = [(1 << 20) // math.isqrt(standing ** slope) + 1 for standing in range(2, count + 1)]
    spare, counts = total - most - (count - 1), [1] * (count - 1)
    while spare > 0:
        candidates = [i for i in range(count - 1) if counts[i] < most]
        pool, left = sum([portions[i] for i in candidates]), spare
        for i in candidates:
            more = min(most - counts[i], max(1, left * portions[i] // pool), spare)
            counts[i] = counts[i] + more
            spare = spare - more
    return np.array([most] + counts)


def uneven_parts(own_key, count, total, most, skew):
    if count == 2:
        one = jax.random.randint(own_key, (), max(1, total - most), min(most, total - 1) + 1)
        return jnp.stack([one, total - one])
    tallies = jnp.asarray(profile(count, total, most, skew), jnp.int32)
    pairs = (count - 1) // 2
    giver, taker = tallies[1:1 + 2 * pairs:2], tallies[2:2 + 2 * pairs:2]
    room = jnp.minimum(giver - 1, most - taker)
    moved = jax.random.randint(jax.random.fold_in(own_key, 1), (pairs,), 0, 1 << 20) % (room + 1)
    tallies = tallies.at[1:1 + 2 * pairs:2].set(giver - moved).at[2:2 + 2 * pairs:2].set(taker + moved)
    return tallies[jax.random.permutation(jax.random.fold_in(own_key, 2), count)]


def bell_draw(own_key, shape, scale, limit, cuts=(), kind=jnp.bfloat16):
    drawn = scale * jax.random.normal(own_key, shape, jnp.float32)
    if cuts:
        drawn = drawn * block_levels(own_key, shape, cuts, -0.22, 0.18)
    return jnp.clip(drawn, -limit, limit).astype(kind)


def setup_inputs(seed: int = 0, part: int = 0) -> dict:
    key_of = jax.random.split(jax.random.key(seed), 8)
    part_splits = jax.random.split(jax.random.fold_in(key_of[7], part), 8)
    return {
        "latents": bell_draw(part_splits[0], (FRAMES * HL, CLAT, WL), 1.0, 6.0, ((0, 16),)),
        "clip_index": jnp.searchsorted(jnp.cumsum(uneven_parts(part_splits[1], CLIPS, FRAMES, CLIP_MOST, 1)), jnp.arange(FRAMES), side="right").astype(jnp.int32),
        "first_conv": bell_draw(key_of[2], (3, 3, 3, CLAT, CH), (27 * CLAT) ** -0.5, 0.3125),
        "first_gain": jnp.clip(1.0 + 0.12 * jax.random.normal(key_of[3], (CH,), jnp.float32), 0.4, 1.6),
        "middle_conv": bell_draw(key_of[4], (3, 3, 3, CH, CH), (27 * CH) ** -0.5, 0.0625),
        "head_gain": jnp.clip(1.0 + 0.12 * jax.random.normal(key_of[5], (CH,), jnp.float32), 0.4, 1.6),
        "head_weight": bell_draw(key_of[6], (CH, 3 * PATCH), CH ** -0.5, 0.3125),
    }


def causal_conv(field, clip_index, weight):
    frames, height, width, channels = field.shape
    outs = weight.shape[-1]
    ids = jnp.concatenate([jnp.full((2,), -1, jnp.int32), clip_index.astype(jnp.int32)])
    padded = jnp.pad(field, ((2, 0), (1, 1), (1, 1), (0, 0)))
    total = jnp.zeros((frames * height * width, outs), jnp.float32)
    for step_t in range(3):
        keep = (ids[step_t:step_t + frames] == ids[2:]).astype(field.dtype)
        slab = padded[step_t:step_t + frames] * keep[:, None, None, None]
        for step_r in range(3):
            rows = slab[:, step_r:step_r + height]
            stacked = jnp.concatenate([rows[:, :, step_c:step_c + width] for step_c in range(3)], axis=-1)
            stacked = stacked.reshape(-1, 3 * channels)
            total = total + jnp.dot(stacked, weight[step_t, step_r].reshape(3 * channels, outs), preferred_element_type=jnp.float32)
    return total.reshape(frames, height, width, outs)

def norm_act(values, gain):
    scale = lax.rsqrt(lax.optimization_barrier(jnp.mean(values * values, axis=-1, keepdims=True)) + 1e-06)
    return jax.nn.silu(values * scale * gain.astype(jnp.float32))

def reference(latents, clip_index, first_conv, first_gain, middle_conv, head_gain, head_weight):
    video = latents.reshape(FRAMES, HL, CLAT, WL).transpose(0, 1, 3, 2)
    first = causal_conv(video, clip_index, first_conv).astype(jnp.bfloat16)
    active = norm_act(first.astype(jnp.float32), first_gain).astype(jnp.bfloat16)
    summed = first.astype(jnp.float32) + causal_conv(active, clip_index, middle_conv)
    outward = norm_act(summed, head_gain).astype(jnp.bfloat16)
    patch = jnp.dot(outward.reshape(-1, CH), head_weight, preferred_element_type=jnp.float32)
    patch = patch.reshape(FRAMES, HL, WL, 3, PATCH)
    half = PATCH // 2
    front = patch[..., :half]
    back = patch[..., half:]
    moved = jnp.concatenate([jnp.zeros_like(back[:, :, :1]), back[:, :, :-1]], axis=2)
    picture = front + moved
    tiles = picture.reshape(BLOCKS, TF, HL, STRIPS, WS, 3, half)
    tiles = tiles.transpose(0, 3, 1, 5, 2, 4, 6)
    tiles = tiles.reshape(TILES, TF, 3, HL, WS * half)
    return jnp.roll(tiles, STRIPS // 2 - 1, axis=0)
```

```python
import functools

import jax
import jax.numpy as jnp
from jax import lax
from jax.experimental import pallas as pl
from jax.experimental.pallas import tpu as pltpu
from jax.sharding import PartitionSpec as P

WS = 16
TF = 2
LANES = 128
GAP = LANES // 2
WIDE = WS + 5
HALF = (WIDE + 1) // 2
PAIRS = (WS + 2) // 2
CHUNK = 16


def norm_act(x, gain):
    scale = lax.rsqrt(jnp.mean(x * x, axis=-1, keepdims=True) + 1e-06)
    h = x * scale * (0.5 * gain)
    return h + h * jnp.tanh(h)


def row_shift(x, by):
    rows = lax.broadcasted_iota(jnp.int32, x.shape, 0)
    n = x.shape[0]
    if by > 0:
        return jnp.where(rows == 0, 0.0, pltpu.roll(x, 1, 0))
    return jnp.where(rows == n - 1, 0.0, pltpu.roll(x, n - 1, 0))


def tap_sums(g):
    ends = g[0] + g[2]
    return [g[0], ends + g[1], ends - g[1], g[2]]


def pair_outputs(m):
    return m[0] + 0.5 * (m[1] + m[2]), 0.5 * (m[1] - m[2]) - m[3]


def exchange_kernel(
    sizes, lat_hbm, wm_hbm, w1_hbm, got, u_ref, w1_ref,
    lat_ref, pad_a, pad_b, packed, stage, raw, send_sem, recv_sem, own_sem, lat_sem, wm_sem, w1_sem,
):
    tiles, strips, frames, shard_rows = sizes
    quarters = tiles // frames
    blocks = tiles // strips
    offset = strips // 2 - 1
    me = lax.axis_index("tile")
    fetch = pltpu.make_async_copy(lat_hbm, lat_ref, lat_sem)
    fetch.start()
    ch = raw.shape[-1]
    group = w1_hbm.shape[1] // 3
    weights = [pltpu.make_async_copy(wm_hbm.at[dt], raw.at[dt], wm_sem.at[dt]) for dt in range(3)]
    inputs = [
        pltpu.make_async_copy(
            w1_hbm.at[dt, pl.ds(dr * group, group)],
            w1_ref.at[dt, pl.ds(dr * GAP, group)],
            w1_sem.at[3 * dt + dr],
        )
        for dt in range(3)
        for dr in range(3)
    ]
    for copy in weights + inputs:
        copy.start()
    barrier = pltpu.get_barrier_semaphore()
    for step in range(1, tiles):
        pl.semaphore_signal(barrier, inc=1, device_id={"tile": lax.rem(me + step, tiles)})

    wl = lat_ref.shape[1]
    fetch.wait()
    values = lat_ref[...].astype(jnp.float32)
    spare = jnp.zeros((2 * LANES - values.shape[0], wl), jnp.float32)
    for pad, rows in ((pad_a, values[:LANES]), (pad_b, jnp.concatenate([values[LANES:], spare]))):
        pad[:8] = jnp.zeros((8, LANES), jnp.float32)
        pad[8 + wl :] = jnp.zeros((WS, LANES), jnp.float32)
        pad[8 : 8 + wl] = rows.T
    low = lax.broadcasted_iota(jnp.int32, (HALF, LANES), 1) < LANES // 2
    for s in range(strips):
        at = WS * s + 8 - 3
        packed[s, :WIDE] = pad_a[at : at + WIDE]
        upper = pltpu.roll(pad_b[at + HALF : at + 2 * HALF], LANES // 2, 1)
        packed[s, WIDE:] = jnp.where(low, pad_b[at : at + HALF], upper)
        stage[s] = packed[s].astype(jnp.bfloat16)
    pl.semaphore_wait(barrier, tiles - 1)

    frame = me // quarters
    quarter = me % quarters

    def each_send(act):
        for ahead in range(3):
            block = frame // TF + ahead
            slot = (2 * TF - TF * ahead + frame % TF) * quarters + quarter

            @pl.when(block < blocks)
            def _():
                @pl.loop(0, strips)
                def _(j):
                    s = (j + me) % strips
                    to = (block * strips + s + offset) % tiles

                    @pl.when(to != me)
                    def _():
                        act(
                            pltpu.make_async_remote_copy(
                                src_ref=stage.at[s],
                                dst_ref=got.at[slot],
                                send_sem=send_sem.at[ahead * strips + s],
                                recv_sem=recv_sem.at[slot],
                                device_id={"tile": to},
                            ),
                            None,
                        )

                    @pl.when(to == me)
                    def _():
                        act(None, pltpu.make_async_copy(stage.at[s], got.at[slot], own_sem))

    def start(remote, local):
        (remote if local is None else local).start()

    def finish(remote, local):
        if local is None:
            remote.wait_send()
        else:
            local.wait()

    each_send(start)

    for dt in range(3):
        for dr in range(3):
            end = (dr + 1) * GAP if dr < 2 else w1_ref.shape[1]
            w1_ref[dt, dr * GAP + group : end] = jnp.zeros((end - dr * GAP - group, ch), jnp.bfloat16)
    for dt in range(3):
        weights[dt].wait()

        @pl.loop(0, ch // CHUNK)
        def _(step, dt=dt):
            rows = pl.ds(pl.multiple_of(step * CHUNK, CHUNK), CHUNK)
            for at in range(0, ch, LANES):
                cols = pl.ds(at, LANES)
                across = [
                    tap_sums([raw[dt, dr, dc, rows, cols].astype(jnp.float32) for dr in range(3)])
                    for dc in range(3)
                ]
                for i in range(4):
                    for j, value in enumerate(tap_sums([across[dc][i] for dc in range(3)])):
                        u_ref[4 * i + j, dt, rows, cols] = value.astype(jnp.bfloat16)

    for copy in inputs:
        copy.wait()
    mine = (me + tiles - offset) % tiles // strips

    @pl.loop(0, 3 * TF * quarters)
    def _(slot):
        source = (TF * mine - 2 * TF) * quarters + slot

        @pl.when(jnp.logical_and(source >= 0, source != me))
        def _():
            pltpu.make_async_remote_copy(
                src_ref=stage.at[0],
                dst_ref=got.at[slot],
                send_sem=send_sem.at[0],
                recv_sem=recv_sem.at[slot],
                device_id={"tile": me},
            ).wait_recv()

    each_send(finish)


def decode_kernel(
    sizes, clip, got_ref, w1_ref, g1_ref, u_ref, g2_ref, hw_ref, out_ref,
    v_ref, r_ref, firstb, fscr, y_ref, outw, main, tail, rowtap, z_ref,
):
    tiles, strips, hl, clat, shard_rows = sizes
    ch = g1_ref.shape[-1]
    patch = hw_ref.shape[0] // 3
    half = patch // 2
    aw = WS + 3
    ow = WS + 1
    hh = hl // 2
    lanes = WS * half
    rotated = (lax.axis_index("tile") + tiles - (strips // 2 - 1)) % tiles
    strip = rotated % strips
    block = rotated // strips
    scal = []
    for i in range(3 * TF):
        at = block * TF - 2 * TF + i
        scal.append(jnp.where(at < 0, -1, clip[jnp.maximum(at, 0)]))
    g1 = g1_ref[...].reshape(1, ch)
    g2 = g2_ref[...].reshape(1, ch)

    wide = rowtap.shape[0] // (hl + 2)
    rowtap[:wide] = jnp.zeros((wide, LANES), jnp.float32)
    rowtap[(hl + 1) * wide :] = jnp.zeros((wide, LANES), jnp.float32)
    at_lane = lax.broadcasted_iota(jnp.int32, (wide, LANES), 1)
    quarters = hl // shard_rows
    per = LANES // clat

    for f in range(3 * TF):

        @pl.when(block * TF - 2 * TF + f < 0)
        def _(f=f):
            z_ref[f] = jnp.zeros(z_ref.shape[1:], jnp.bfloat16)

        @pl.when(block * TF - 2 * TF + f >= 0)
        def _(f=f):
            for q in range(quarters):
                main[q] = got_ref[f * quarters + q].astype(jnp.float32)
                tail[q, :HALF] = main[q, WIDE:]
                tail[q, HALF : 2 * HALF] = pltpu.roll(main[q, WIDE:], LANES // 2, 1)
                for first_row, count, x in ((0, per, main.at[q]), (per, shard_rows - per, tail.at[q])):
                    shifts = [x[dc : dc + wide] for dc in range(3)]
                    for r in range(count):
                        y = jnp.zeros((wide, LANES), jnp.float32)
                        for dc in (2, 1, 0):
                            turn = (dc - r) * clat % LANES
                            moved = pltpu.roll(shifts[dc], turn, 1) if turn else shifts[dc]
                            y = jnp.where(at_lane < (dc + 1) * clat, moved, y)
                        start = (1 + q * shard_rows + first_row + r) * wide
                        rowtap[start : start + wide] = y

            for w in range(aw):
                v = [rowtap[pl.ds(k * wide + w, hh, stride=2 * wide), :] for k in range(4)]
                turned = [pltpu.roll(v[k], GAP, 1) for k in (1, 2)]
                low = jnp.concatenate([v[0] + turned[0], v[1] + turned[1]])
                z_ref[f, w, :, :LANES] = low.astype(jnp.bfloat16)
                z_ref[f, w, :, LANES:] = jnp.concatenate(v[2:]).astype(jnp.bfloat16)

    for f in range(TF + 2):
        if f == 0:
            needed = scal[2] == scal[4]
        elif f == 1:
            needed = jnp.logical_or(scal[3] == scal[4], scal[3] == scal[5])
        else:
            needed = scal[4] == scal[4]

        @pl.when(needed)
        def _(f=f):
            taps = []
            for dt in range(3):
                keep = (scal[f + dt] == scal[f + 2]).astype(jnp.float32)
                lhs = z_ref[f + dt].reshape(aw * hl, z_ref.shape[-1])
                taps.append(lhs * keep.astype(jnp.bfloat16) if dt < 2 else lhs)
            fscr[...] = jnp.dot(
                jnp.concatenate(taps, axis=-1), w1_ref[...].reshape(-1, ch),
                preferred_element_type=jnp.float32,
            ).reshape(aw, hl, ch)

            for w in range(aw):
                rounded = fscr[w].astype(jnp.bfloat16)
                if f >= 2:
                    firstb[f - 2, w] = rounded
                value = norm_act(rounded.astype(jnp.float32), g1)
                if w < 2:
                    value = value * (strip > 0).astype(jnp.float32)
                if w == aw - 1:
                    value = value * (strip < strips - 1).astype(jnp.float32)
                even, odd = value[:hh], value[hh:]
                r_ref[w, 0] = row_shift(odd, 1) - odd
                r_ref[w, 1] = even + odd
                r_ref[w, 2] = odd - even
                r_ref[w, 3] = even - row_shift(even, -1)

            for c in range(0, PAIRS, 2):
                for i in range(4):
                    d = [r_ref[2 * c + k, i] for k in range(min(6, aw - 2 * c))]
                    cells = [[d[0] - d[2], d[1] + d[2], d[2] - d[1], d[1] - d[3] if len(d) > 3 else d[1]]]
                    if c + 1 < PAIRS:
                        cells.append([d[2] - d[4], d[3] + d[4], d[4] - d[3], d[3] - d[5]])
                    else:
                        cells.append([jnp.zeros((8, ch), jnp.float32)] * 4)
                    for j in range(4):
                        both = jnp.concatenate([cell[j] for cell in cells])
                        v_ref[f, 4 * i + j, c * hh : c * hh + both.shape[0]] = both.astype(jnp.bfloat16)

    same12 = scal[3] == scal[4]
    same23 = scal[4] == scal[5]

    def products(first_taps, second_taps):
        @pl.loop(0, 4)
        def _(i):
            sums = []
            for j in range(4):
                comp = 4 * i + j
                sums.append([
                    jnp.dot(
                        jnp.concatenate([v_ref[a, comp] for a, _ in taps], axis=-1),
                        jnp.concatenate([u_ref[comp, dt] for _, dt in taps], axis=0),
                        preferred_element_type=jnp.float32,
                    )
                    for taps in (first_taps, second_taps)
                ])
            for fo in range(TF):
                y_ref[fo, i, 0], y_ref[fo, i, 1] = pair_outputs([s[fo] for s in sums])

    @pl.when(jnp.logical_and(same12, same23))
    def _():
        @pl.loop(0, 4)
        def _(i):
            sums = []
            for j in range(4):
                comp = 4 * i + j
                both = jnp.dot(
                    jnp.concatenate([v_ref[1, comp], v_ref[2, comp]], axis=-1),
                    jnp.concatenate([
                        jnp.concatenate([u_ref[comp, 1], u_ref[comp, 0]], axis=-1),
                        jnp.concatenate([u_ref[comp, 2], u_ref[comp, 1]], axis=-1),
                    ], axis=0),
                    preferred_element_type=jnp.float32,
                )
                last = jnp.dot(v_ref[3, comp], u_ref[comp, 2], preferred_element_type=jnp.float32)
                sums.append([both[:, :ch], both[:, ch:] + last])
            for fo in range(TF):
                y_ref[fo, i, 0], y_ref[fo, i, 1] = pair_outputs([s[fo] for s in sums])

    @pl.when(jnp.logical_and(same12, jnp.logical_not(same23)))
    def _():
        products([(1, 1), (2, 2)], [(3, 2)])

    @pl.when(jnp.logical_and(jnp.logical_not(same12), same23))
    def _():
        products([(2, 2)], [(2, 1), (3, 2)])

    @pl.when(jnp.logical_and(jnp.logical_not(same12), jnp.logical_not(same23)))
    def _():
        products([(2, 2)], [(3, 2)])

    @pl.when(scal[2] == scal[4])
    def _():
        @pl.loop(0, 4)
        def _(i):
            sums = [
                jnp.dot(v_ref[0, 4 * i + j], u_ref[4 * i + j, 0], preferred_element_type=jnp.float32)
                for j in range(4)
            ]
            front, back = pair_outputs(sums)
            y_ref[0, i, 0] += front
            y_ref[0, i, 1] += back

    rows = lax.broadcasted_iota(jnp.int32, (3 * patch, 6 * lanes), 0)
    cols = lax.broadcasted_iota(jnp.int32, (3 * patch, 6 * lanes), 1)
    odd = cols // (3 * lanes)
    colour = (cols // lanes) % 3
    want = colour * patch + (cols % lanes + half * odd) % patch
    spread = (rows == want).astype(jnp.bfloat16)
    head = lax.dot_general(
        hw_ref[...], spread, (((0,), (0,)), ((), ())), preferred_element_type=jnp.float32
    ).astype(jnp.bfloat16)
    lane = lax.broadcasted_iota(jnp.int32, (hl, lanes), 1)

    for fo in range(TF):
        for w in range(ow):
            part = pl.ds(w // 2 * hh, hh)
            added = jnp.concatenate(pair_outputs([y_ref[fo, i, w % 2, part] for i in range(4)]))
            value = norm_act(firstb[fo, w + 1].astype(jnp.float32) + added, g2)
            if w == 0:
                value = value * (strip > 0).astype(jnp.float32)
            outw[fo, w % 2, w // 2] = value.astype(jnp.bfloat16)

        p_odd = jnp.dot(
            outw[fo, 0].reshape(-1, ch), head[:, 3 * lanes :], preferred_element_type=jnp.float32
        )
        p_even = jnp.dot(
            outw[fo, 1, : WS // 2].reshape(-1, ch), head[:, : 3 * lanes],
            preferred_element_type=jnp.float32,
        )
        for k in range(3):
            front = jnp.zeros((hl, lanes), jnp.float32)
            back = jnp.zeros((hl, lanes), jnp.float32)
            for i in range(WS // 2):
                piece = p_even[i * hl : (i + 1) * hl, k * lanes : (k + 1) * lanes]
                front = jnp.where(lane // patch == i, piece, front)
            for i in range(WS // 2 + 1):
                piece = p_odd[i * hl : (i + 1) * hl, k * lanes : (k + 1) * lanes]
                back = jnp.where((lane + half) // patch == i, piece, back)
            out_ref[fo, k, pl.ds(0, hh, stride=2), :] = (front + back)[:hh]
            out_ref[fo, k, pl.ds(1, hh, stride=2), :] = (front + back)[hh:]


def decode_call(sizes, patch, ch, operands):
    tiles, strips, hl, clat, shard_rows = sizes
    quarters = hl // shard_rows
    aw = WS + 3
    half = patch // 2
    mrows = -(-PAIRS * (hl // 2) // 16) * 16
    vm = pl.BlockSpec(memory_space=pltpu.VMEM)
    return pl.pallas_call(
        functools.partial(decode_kernel, sizes),
        out_shape=jax.ShapeDtypeStruct((TF, 3, hl, WS * half), jnp.float32),
        in_specs=[pl.BlockSpec(memory_space=pltpu.SMEM)] + [vm] * 6,
        out_specs=vm,
        scratch_shapes=[
            pltpu.VMEM((TF + 2, 16, mrows, ch), jnp.bfloat16),
            pltpu.VMEM((aw, 4, hl // 2, ch), jnp.float32),
            pltpu.VMEM((TF, aw, hl, ch), jnp.bfloat16),
            pltpu.VMEM((aw, hl, ch), jnp.float32),
            pltpu.VMEM((TF, 4, 2, mrows, ch), jnp.float32),
            pltpu.VMEM((TF, 2, WS // 2 + 1, hl, ch), jnp.bfloat16),
            pltpu.VMEM((quarters, WIDE + HALF, LANES), jnp.float32),
            pltpu.VMEM((quarters, WIDE + HALF, LANES), jnp.float32),
            pltpu.VMEM(((hl + 2) * 24, LANES), jnp.float32),
            pltpu.VMEM((3 * TF, aw, hl, 2 * LANES), jnp.bfloat16),
        ],
        compiler_params=pltpu.CompilerParams(vmem_limit_bytes=44 * 1024 * 1024),
    )(*operands)


def per_device(latents, clip_index, first_conv, first_gain, middle_conv, head_gain, head_weight):
    tiles = lax.axis_size("tile")
    shard_rows, clat, wl = latents.shape
    ch = first_gain.shape[0]
    frames = clip_index.shape[0]
    hl = tiles * shard_rows // frames
    strips = wl // WS
    quarters = tiles // frames
    slots = 3 * TF * quarters
    vm = pl.BlockSpec(memory_space=pltpu.VMEM)
    got, sums, first_taps = pl.pallas_call(
        functools.partial(exchange_kernel, (tiles, strips, frames, shard_rows)),
        out_shape=[
            pltpu.VMEM((slots, WIDE + HALF, LANES), jnp.bfloat16),
            pltpu.VMEM((16, 3, ch, ch), jnp.bfloat16),
            pltpu.VMEM((3, 2 * LANES, ch), jnp.bfloat16),
        ],
        in_specs=[pl.BlockSpec(memory_space=pl.ANY)] * 3,
        out_specs=[vm] * 3,
        scratch_shapes=[
            pltpu.VMEM((shard_rows * clat, wl), jnp.bfloat16),
            pltpu.VMEM((8 + wl + WS, LANES), jnp.float32),
            pltpu.VMEM((8 + wl + WS, LANES), jnp.float32),
            pltpu.VMEM((strips, WIDE + HALF, LANES), jnp.float32),
            pltpu.VMEM((strips, WIDE + HALF, LANES), jnp.bfloat16),
            pltpu.VMEM((3, 3, 3, ch, ch), jnp.bfloat16),
            pltpu.SemaphoreType.DMA((3 * strips,)),
            pltpu.SemaphoreType.DMA((slots,)),
            pltpu.SemaphoreType.DMA,
            pltpu.SemaphoreType.DMA,
            pltpu.SemaphoreType.DMA((3,)),
            pltpu.SemaphoreType.DMA((9,)),
        ],
        compiler_params=pltpu.CompilerParams(
            collective_id=0, has_side_effects=True, vmem_limit_bytes=44 * 1024 * 1024
        ),
    )(latents.reshape(shard_rows * clat, wl), middle_conv, first_conv.reshape(3, 9 * clat, ch))
    got, sums, first_taps = [
        pltpu.with_memory_space_constraint(x, pltpu.VMEM) for x in (got, sums, first_taps)
    ]
    out = decode_call(
        (tiles, strips, hl, clat, shard_rows), head_weight.shape[1] // 3, ch,
        (clip_index, got, first_taps, first_gain, sums, head_gain, head_weight.T),
    )
    return out[None]


def solution(mesh):
    placed = (P(("group", "tile"), None, None), P("group"), P(), P(), P(), P(), P())
    return jax.shard_map(
        per_device,
        mesh=mesh,
        in_specs=placed,
        out_specs=P(("group", "tile"), None, None, None, None),
        check_vma=False,
    )
```

```python
import functools

import jax
import jax.numpy as jnp
from jax import lax
from jax.experimental import pallas as pl
from jax.experimental.pallas import tpu as pltpu
from jax.sharding import PartitionSpec as P

WS = 16
TF = 2
LANES = 128
GAP = LANES // 2
WIDE = WS + 5
HALF = (WIDE + 1) // 2
PAIRS = (WS + 2) // 2
CHUNK = 16


def norm_act(x, gain):
    scale = lax.rsqrt(jnp.mean(x * x, axis=-1, keepdims=True) + 1e-06)
    h = x * scale * (0.5 * gain)
    return h + h * jnp.tanh(h)


def row_shift(x, by):
    rows = lax.broadcasted_iota(jnp.int32, x.shape, 0)
    n = x.shape[0]
    if by > 0:
        return jnp.where(rows == 0, 0.0, pltpu.roll(x, 1, 0))
    return jnp.where(rows == n - 1, 0.0, pltpu.roll(x, n - 1, 0))


def tap_sums(g):
    ends = g[0] + g[2]
    return [g[0], ends + g[1], ends - g[1], g[2]]


def pair_outputs(m):
    return m[0] + 0.5 * (m[1] + m[2]), 0.5 * (m[1] - m[2]) - m[3]


def exchange_kernel(
    sizes, lat_hbm, wm_hbm, w1_hbm, got, u_ref, w1_ref,
    lat_ref, pad_a, pad_b, packed, stage, raw, send_sem, recv_sem, own_sem, lat_sem, wm_sem, w1_sem,
):
    tiles, strips, frames, shard_rows = sizes
    quarters = tiles // frames
    blocks = tiles // strips
    offset = strips // 2 - 1
    me = lax.axis_index("tile")
    fetch = pltpu.make_async_copy(lat_hbm, lat_ref, lat_sem)
    fetch.start()
    ch = raw.shape[-1]
    group = w1_hbm.shape[1] // 3
    weights = [pltpu.make_async_copy(wm_hbm.at[dt], raw.at[dt], wm_sem.at[dt]) for dt in range(3)]
    inputs = [
        pltpu.make_async_copy(
            w1_hbm.at[dt, pl.ds(dr * group, group)],
            w1_ref.at[dt, pl.ds(dr * GAP, group)],
            w1_sem.at[3 * dt + dr],
        )
        for dt in range(3)
        for dr in range(3)
    ]
    for copy in weights + inputs:
        copy.start(priority=1)
    barrier = pltpu.get_barrier_semaphore()
    for step in range(1, tiles):
        pl.semaphore_signal(barrier, inc=1, device_id={"tile": lax.rem(me + step, tiles)})

    wl = lat_ref.shape[1]
    fetch.wait()
    values = lat_ref[...].astype(jnp.float32)
    spare = jnp.zeros((2 * LANES - values.shape[0], wl), jnp.float32)
    for pad, rows in ((pad_a, values[:LANES]), (pad_b, jnp.concatenate([values[LANES:], spare]))):
        pad[:8] = jnp.zeros((8, LANES), jnp.float32)
        pad[8 + wl :] = jnp.zeros((WS, LANES), jnp.float32)
        pad[8 : 8 + wl] = rows.T
    low = lax.broadcasted_iota(jnp.int32, (HALF, LANES), 1) < LANES // 2
    for s in range(strips):
        at = WS * s + 8 - 3
        packed[s, :WIDE] = pad_a[at : at + WIDE]
        upper = pltpu.roll(pad_b[at + HALF : at + 2 * HALF], LANES // 2, 1)
        packed[s, WIDE:] = jnp.where(low, pad_b[at : at + HALF], upper)
        stage[s] = packed[s].astype(jnp.bfloat16)
    pl.semaphore_wait(barrier, tiles - 1)

    frame = me // quarters
    quarter = me % quarters

    def each_send(act):
        for ahead in range(3):
            block = frame // TF + ahead
            slot = (2 * TF - TF * ahead + frame % TF) * quarters + quarter

            @pl.when(block < blocks)
            def _():
                @pl.loop(0, strips)
                def _(j):
                    s = (j + me) % strips
                    to = (block * strips + s + offset) % tiles

                    @pl.when(to != me)
                    def _():
                        act(
                            pltpu.make_async_remote_copy(
                                src_ref=stage.at[s],
                                dst_ref=got.at[slot],
                                send_sem=send_sem.at[ahead * strips + s],
                                recv_sem=recv_sem.at[slot],
                                device_id={"tile": to},
                            ),
                            None,
                        )

                    @pl.when(to == me)
                    def _():
                        act(None, pltpu.make_async_copy(stage.at[s], got.at[slot], own_sem))

    def start(remote, local):
        (remote if local is None else local).start()

    def finish(remote, local):
        if local is None:
            remote.wait_send()
        else:
            local.wait()

    each_send(start)

    for dt in range(3):
        for dr in range(3):
            end = (dr + 1) * GAP if dr < 2 else w1_ref.shape[1]
            w1_ref[dt, dr * GAP + group : end] = jnp.zeros((end - dr * GAP - group, ch), jnp.bfloat16)
    for dt in range(3):
        weights[dt].wait()

        @pl.loop(0, ch // CHUNK)
        def _(step, dt=dt):
            rows = pl.ds(pl.multiple_of(step * CHUNK, CHUNK), CHUNK)
            for at in range(0, ch, LANES):
                cols = pl.ds(at, LANES)
                across = [
                    tap_sums([raw[dt, dr, dc, rows, cols].astype(jnp.float32) for dr in range(3)])
                    for dc in range(3)
                ]
                for i in range(4):
                    for j, value in enumerate(tap_sums([across[dc][i] for dc in range(3)])):
                        u_ref[4 * i + j, dt, rows, cols] = value.astype(jnp.bfloat16)

    for copy in inputs:
        copy.wait()
    mine = (me + tiles - offset) % tiles // strips

    @pl.loop(0, 3 * TF * quarters)
    def _(slot):
        source = (TF * mine - 2 * TF) * quarters + slot

        @pl.when(jnp.logical_and(source >= 0, source != me))
        def _():
            pltpu.make_async_remote_copy(
                src_ref=stage.at[0],
                dst_ref=got.at[slot],
                send_sem=send_sem.at[0],
                recv_sem=recv_sem.at[slot],
                device_id={"tile": me},
            ).wait_recv()

    each_send(finish)


def decode_kernel(
    sizes, clip, got_ref, w1_ref, g1_ref, u_ref, g2_ref, hw_ref, out_ref,
    v_ref, v3_ref, va_ref, vb_ref, r_ref, firstb, fscr, ya_ref, yb_ref, outw, head_ref, main, tail, rowtap, z_ref,
):
    tiles, strips, hl, clat, shard_rows = sizes
    ch = g1_ref.shape[-1]
    patch = hw_ref.shape[0] // 3
    half = patch // 2
    aw = WS + 3
    ow = WS + 1
    hh = hl // 2
    lanes = WS * half
    rotated = (lax.axis_index("tile") + tiles - (strips // 2 - 1)) % tiles
    strip = rotated % strips
    block = rotated // strips

    def clip_of(i):
        at = block * TF - 2 * TF + i
        return jnp.where(at < 0, -1, clip[jnp.maximum(at, 0)])

    scal = [clip_of(i) for i in range(3 * TF)]
    g1 = g1_ref[...].reshape(1, ch)
    g2 = g2_ref[...].reshape(1, ch)

    wide = rowtap.shape[0] // (hl + 2)
    rowtap[:wide] = jnp.zeros((wide, LANES), jnp.float32)
    rowtap[(hl + 1) * wide :] = jnp.zeros((wide, LANES), jnp.float32)
    at_lane = lax.broadcasted_iota(jnp.int32, (wide, LANES), 1)
    quarters = hl // shard_rows
    per = LANES // clat

    same12 = scal[3] == scal[4]
    same23 = scal[4] == scal[5]
    same02 = scal[2] == scal[4]
    for f in range(3 * TF):

        @pl.when(scal[f] == scal[4] if f < 4 else block >= 0)
        def _(f=f):
            for q in range(quarters):
                main[q] = got_ref[f * quarters + q].astype(jnp.float32)
                tail[q, :HALF] = main[q, WIDE:]
                tail[q, HALF : 2 * HALF] = pltpu.roll(main[q, WIDE:], LANES // 2, 1)
                for first_row, count, x in ((0, per, main.at[q]), (per, shard_rows - per, tail.at[q])):
                    shifts = [x[dc : dc + wide] for dc in range(3)]
                    for r in range(count):
                        y = jnp.zeros((wide, LANES), jnp.float32)
                        for dc in (2, 1, 0):
                            turn = (dc - r) * clat % LANES
                            moved = pltpu.roll(shifts[dc], turn, 1) if turn else shifts[dc]
                            y = jnp.where(at_lane < (dc + 1) * clat, moved, y)
                        start = (1 + q * shard_rows + first_row + r) * wide
                        rowtap[start : start + wide] = y

            for w in range(aw):
                v = [rowtap[pl.ds(k * wide + w, hh, stride=2 * wide), :] for k in range(4)]
                turned = [pltpu.roll(v[k], GAP, 1) for k in (1, 2)]
                low = jnp.concatenate([v[0] + turned[0], v[1] + turned[1]])
                z_ref[f, w, :, :LANES] = low.astype(jnp.bfloat16)
                z_ref[f, w, :, LANES:] = jnp.concatenate(v[2:]).astype(jnp.bfloat16)

    def first_dot(f, keeps, at):
        count = len(keeps)
        taps = [z_ref[f + 3 - count + k].reshape(aw * hl, -1) for k in range(count)]
        taps = [x if keep is None else jnp.where(keep, x, 0) for x, keep in zip(taps, keeps)]
        fscr[at] = jnp.dot(
            jnp.concatenate(taps, axis=-1), w1_ref[3 - count :].reshape(-1, ch),
            preferred_element_type=jnp.float32,
        ).reshape(aw, hl, ch)

    def first_norm(f, w, at, inside):
        rounded = fscr[at, w].astype(jnp.bfloat16)
        if not isinstance(f, int):
            firstb[jnp.maximum(f - 2, 0), w] = rounded
        elif f >= 2:
            firstb[f - 2, w] = rounded
        value = norm_act(rounded.astype(jnp.float32), g1)
        if inside is not None:
            value = value * inside.astype(jnp.float32)
        even, odd = value[:hh], value[hh:]
        r_ref[f, w, 0] = row_shift(odd, 1) - odd
        r_ref[f, w, 1] = even + odd
        r_ref[f, w, 2] = odd - even
        r_ref[f, w, 3] = even - row_shift(even, -1)

    def first(f, *keeps):
        first_dot(f, keeps, f % 2)
        for w in range(aw):
            first_norm(f, w, f % 2, strip > 0 if w < 2 else strip < strips - 1 if w == aw - 1 else None)

    def expand(f, i, dst):
        for c in range(0, PAIRS, 2):
            d = [r_ref[f, 2 * c + k, i] for k in range(min(6, aw - 2 * c))]
            cells = [[d[0] - d[2], d[1] + d[2], d[2] - d[1], d[1] - d[3] if len(d) > 3 else d[1]]]
            if c + 1 < PAIRS:
                cells.append([d[2] - d[4], d[3] + d[4], d[4] - d[3], d[3] - d[5]])
            else:
                cells.append([jnp.zeros((8, ch), jnp.float32)] * 4)
            for j in range(4):
                both = jnp.concatenate([cell[j] for cell in cells])
                dst[j, c * hh : c * hh + both.shape[0]] = both.astype(jnp.bfloat16)

    def product(sides, weights):
        return jnp.dot(
            jnp.concatenate(sides, axis=-1), jnp.concatenate(weights, axis=0),
            preferred_element_type=jnp.float32,
        )

    def product_both(sides, comp):
        w0, w1, w2 = [u_ref[comp, dt] for dt in range(3)]
        return product(
            sides, [jnp.concatenate([w1, w0], axis=-1), jnp.concatenate([w2, w1], axis=-1)]
        )

    def put(y, i, sums):
        y[i, 0], y[i, 1] = pair_outputs(sums)

    def put_more(y, i, sums):
        front, back = pair_outputs(sums)
        y[i, 0] += front
        y[i, 1] += back

    rows = lax.broadcasted_iota(jnp.int32, (3 * patch, 6 * lanes), 0)
    cols = lax.broadcasted_iota(jnp.int32, (3 * patch, 6 * lanes), 1)
    odd = cols // (3 * lanes)
    colour = (cols // lanes) % 3
    want = colour * patch + (cols % lanes + half * odd) % patch
    spread = (rows == want).astype(jnp.bfloat16)
    head_ref[...] = lax.dot_general(
        hw_ref[...], spread, (((0,), (0,)), ((), ())), preferred_element_type=jnp.float32
    ).astype(jnp.bfloat16)
    lane = lax.broadcasted_iota(jnp.int32, (hl, lanes), 1)

    def outward(fo, y, cell, side):
        part = pl.ds(pl.multiple_of(cell * hh, 8), hh)
        added = jnp.concatenate(pair_outputs([y[i, side, part] for i in range(4)]))
        value = norm_act(firstb[fo, 2 * cell + side + 1].astype(jnp.float32) + added, g2)
        if side == 0:
            value = value * jnp.logical_or(cell > 0, strip > 0).astype(jnp.float32)
        outw[side, cell] = value.astype(jnp.bfloat16)

    def picture(fo):
        p_odd = jnp.dot(
            outw[0].reshape(-1, ch), head_ref[:, 3 * lanes :], preferred_element_type=jnp.float32
        )
        p_even = jnp.dot(
            outw[1, : WS // 2].reshape(-1, ch), head_ref[:, : 3 * lanes],
            preferred_element_type=jnp.float32,
        )
        for k in range(3):
            front = jnp.zeros((hl, lanes), jnp.float32)
            back = jnp.zeros((hl, lanes), jnp.float32)
            for i in range(WS // 2):
                piece = p_even[i * hl : (i + 1) * hl, k * lanes : (k + 1) * lanes]
                front = jnp.where(lane // patch == i, piece, front)
            for i in range(WS // 2 + 1):
                piece = p_odd[i * hl : (i + 1) * hl, k * lanes : (k + 1) * lanes]
                back = jnp.where((lane + half) // patch == i, piece, back)
            out_ref[fo, k, pl.ds(0, hh, stride=2), :] = (front + back)[:hh]
            out_ref[fo, k, pl.ds(1, hh, stride=2), :] = (front + back)[hh:]

    late = jnp.logical_not(same02)
    early = jnp.logical_and(jnp.logical_and(same02, jnp.logical_not(same23)), scal[1] != scal[2])

    def all_outward(fo, y):
        for w in range(ow):
            outward(fo, y, w // 2, w % 2)
        picture(fo)

    def halves(body):
        @pl.loop(0, 2)
        def _(pair):
            body(2 * pair, va_ref, vb_ref)
            body(2 * pair + 1, vb_ref, va_ref)

    def quarters_of(body):
        for pair in range(2):
            body(2 * pair, va_ref, vb_ref)
            body(2 * pair + 1, vb_ref, va_ref)

    @pl.when(late)
    def _():
        @pl.when(same12)
        def _():
            first(1, None)

        @pl.when(jnp.logical_not(same12))
        def _():
            r_ref[1] = jnp.zeros(r_ref.shape[1:], jnp.float32)

        first(2, same12, None)
        expand(1, 0, va_ref.at[0])
        expand(2, 0, va_ref.at[1])
        first(3, scal[3] == scal[5], same23, None)
        use_last = same23.astype(jnp.float32)

        def both(i, now, later):
            after = jnp.minimum(i + 1, 3)
            sums = []
            for j in range(4):
                sums.append(product_both([now[0, j], now[1, j]], 4 * i + j))
                if j in (1, 2):
                    expand(j, after, later.at[j - 1])
                if j == 3:
                    expand(3, i, v3_ref.at[pl.ds(4 * i, 4)])
            put(ya_ref, i, [x[:, :ch] for x in sums])
            put(yb_ref, i, [use_last * x[:, ch:] for x in sums])

        def last(i, now, later):
            sums = [product([v3_ref[4 * i + j]], [u_ref[4 * i + j, 2]]) for j in range(4)]
            for k in range(4):
                outward(0, ya_ref, 2 * i + k // 2, k % 2)
            put_more(yb_ref, i, sums)

        halves(both)
        halves(last)
        outward(0, ya_ref, WS // 2, 0)
        picture(0)

    @pl.when(early)
    def _():
        first(3, None)
        first(2, None, None, None)
        for i in range(4):
            expand(3, i, v3_ref.at[pl.ds(4 * i, 4)])
        first(1, None, None)
        first(0, None)

        def alone(i, now, later):
            sums = []
            for j in range(4):
                sums.append(product([v3_ref[4 * i + j]], [u_ref[4 * i + j, 2]]))
                if j < 3:
                    expand(j, i, v_ref.at[j, pl.ds(4 * i, 4)])
            put(ya_ref, i, sums)

        def three(i, now, later):
            sums = [
                product(
                    [v_ref[f, 4 * i + j] for f in range(3)], [u_ref[4 * i + j, dt] for dt in range(3)]
                )
                for j in range(4)
            ]
            for k in range(4):
                outward(1, ya_ref, 2 * i + k // 2, k % 2)
            put(yb_ref, i, sums)

        quarters_of(alone)
        quarters_of(three)
        outward(1, ya_ref, WS // 2, 0)
        picture(1)

    @pl.when(jnp.logical_not(jnp.logical_or(late, early)))
    def _():
        ya_ref[...] = jnp.zeros_like(ya_ref)
        yb_ref[...] = jnp.zeros_like(yb_ref)

        @pl.loop(0, TF + 2)
        def _(f):
            ids = [clip_of(f + dt) for dt in range(3)]
            first_dot(f, [ids[0] == ids[2], ids[1] == ids[2], None], 0)

            @pl.loop(0, aw)
            def _(w):
                first_norm(f, w, 0, ((strip > 0) | (w >= 2)) & ((strip < strips - 1) | (w < aw - 1)))

            @pl.loop(0, 4)
            def _(i):
                expand(f, i, v3_ref.at[pl.ds(4 * i, 4)])

            for fo, y in enumerate((ya_ref, yb_ref)):

                @pl.when(jnp.logical_and(jnp.logical_and(f >= fo, f <= fo + 2), ids[2] == scal[4 + fo]))
                def _(fo=fo, y=y):
                    @pl.loop(0, 4)
                    def _(i):
                        @pl.loop(0, 4)
                        def _(j):
                            one = product([v3_ref[4 * i + j]], [u_ref[4 * i + j, f - fo]])
                            y[i, 0] += jnp.where(j == 0, 1.0, jnp.where(j == 3, 0.0, 0.5)) * one
                            y[i, 1] += jnp.where(j == 0, 0.0, jnp.where(j == 3, -1.0, 1.5 - j)) * one

        all_outward(0, ya_ref)

    all_outward(jnp.where(early, 0, 1), yb_ref)


def decode_call(sizes, patch, ch, operands):
    tiles, strips, hl, clat, shard_rows = sizes
    quarters = hl // shard_rows
    aw = WS + 3
    half = patch // 2
    mrows = -(-PAIRS * (hl // 2) // 16) * 16
    vm = pl.BlockSpec(memory_space=pltpu.VMEM)
    return pl.pallas_call(
        functools.partial(decode_kernel, sizes),
        out_shape=jax.ShapeDtypeStruct((TF, 3, hl, WS * half), jnp.float32),
        in_specs=[pl.BlockSpec(memory_space=pltpu.SMEM)] + [vm] * 6,
        out_specs=vm,
        scratch_shapes=[
            pltpu.VMEM((TF + 1, 16, mrows, ch), jnp.bfloat16),
            pltpu.VMEM((16, mrows, ch), jnp.bfloat16),
            pltpu.VMEM((2, 4, mrows, ch), jnp.bfloat16),
            pltpu.VMEM((2, 4, mrows, ch), jnp.bfloat16),
            pltpu.VMEM((TF + 2, aw, 4, hl // 2, ch), jnp.float32),
            pltpu.VMEM((TF, aw, hl, ch), jnp.bfloat16),
            pltpu.VMEM((2, aw, hl, ch), jnp.float32),
            pltpu.VMEM((4, 2, mrows, ch), jnp.float32),
            pltpu.VMEM((4, 2, mrows, ch), jnp.float32),
            pltpu.VMEM((2, WS // 2 + 1, hl, ch), jnp.bfloat16),
            pltpu.VMEM((ch, 6 * WS * half), jnp.bfloat16),
            pltpu.VMEM((quarters, WIDE + HALF, LANES), jnp.float32),
            pltpu.VMEM((quarters, WIDE + HALF, LANES), jnp.float32),
            pltpu.VMEM(((hl + 2) * 24, LANES), jnp.float32),
            pltpu.VMEM((3 * TF, aw, hl, 2 * LANES), jnp.bfloat16),
        ],
        compiler_params=pltpu.CompilerParams(vmem_limit_bytes=44 * 1024 * 1024),
    )(*operands)


def per_device(latents, clip_index, first_conv, first_gain, middle_conv, head_gain, head_weight):
    tiles = lax.axis_size("tile")
    shard_rows, clat, wl = latents.shape
    ch = first_gain.shape[0]
    frames = clip_index.shape[0]
    hl = tiles * shard_rows // frames
    strips = wl // WS
    quarters = tiles // frames
    slots = 3 * TF * quarters
    vm = pl.BlockSpec(memory_space=pltpu.VMEM)
    got, sums, first_taps = pl.pallas_call(
        functools.partial(exchange_kernel, (tiles, strips, frames, shard_rows)),
        out_shape=[
            pltpu.VMEM((slots, WIDE + HALF, LANES), jnp.bfloat16),
            pltpu.VMEM((16, 3, ch, ch), jnp.bfloat16),
            pltpu.VMEM((3, 2 * LANES, ch), jnp.bfloat16),
        ],
        in_specs=[pl.BlockSpec(memory_space=pl.ANY)] * 3,
        out_specs=[vm] * 3,
        scratch_shapes=[
            pltpu.VMEM((shard_rows * clat, wl), jnp.bfloat16),
            pltpu.VMEM((8 + wl + WS, LANES), jnp.float32),
            pltpu.VMEM((8 + wl + WS, LANES), jnp.float32),
            pltpu.VMEM((strips, WIDE + HALF, LANES), jnp.float32),
            pltpu.VMEM((strips, WIDE + HALF, LANES), jnp.bfloat16),
            pltpu.VMEM((3, 3, 3, ch, ch), jnp.bfloat16),
            pltpu.SemaphoreType.DMA((3 * strips,)),
            pltpu.SemaphoreType.DMA((slots,)),
            pltpu.SemaphoreType.DMA,
            pltpu.SemaphoreType.DMA,
            pltpu.SemaphoreType.DMA((3,)),
            pltpu.SemaphoreType.DMA((9,)),
        ],
        compiler_params=pltpu.CompilerParams(
            collective_id=0, has_side_effects=True, vmem_limit_bytes=44 * 1024 * 1024
        ),
    )(latents.reshape(shard_rows * clat, wl), middle_conv, first_conv.reshape(3, 9 * clat, ch))
    got, sums, first_taps = [
        pltpu.with_memory_space_constraint(x, pltpu.VMEM) for x in (got, sums, first_taps)
    ]
    out = decode_call(
        (tiles, strips, hl, clat, shard_rows), head_weight.shape[1] // 3, ch,
        (clip_index, got, first_taps, first_gain, sums, head_gain, head_weight.T),
    )
    return out[None]


def solution(mesh):
    placed = (P(("group", "tile"), None, None), P("group"), P(), P(), P(), P(), P())
    return jax.shard_map(
        per_device,
        mesh=mesh,
        in_specs=placed,
        out_specs=P(("group", "tile"), None, None, None, None),
        check_vma=False,
    )
```

```python
import functools

import jax
import jax.numpy as jnp
from jax import lax
from jax.experimental import pallas as pl
from jax.experimental.pallas import tpu as pltpu
from jax.sharding import PartitionSpec as P

WS = 16
TF = 2
LANES = 128
GAP = LANES // 2
WIDE = WS + 5
HALF = (WIDE + 1) // 2
PAIRS = (WS + 2) // 2
CHUNK = 16


def norm_act(x, gain):
    scale = lax.rsqrt(jnp.mean(x * x, axis=-1, keepdims=True) + 1e-06)
    h = x * scale * (0.5 * gain)
    return h + h * jnp.tanh(h)


def row_shift(x, by):
    rows = lax.broadcasted_iota(jnp.int32, x.shape, 0)
    n = x.shape[0]
    if by > 0:
        return jnp.where(rows == 0, 0.0, pltpu.roll(x, 1, 0))
    return jnp.where(rows == n - 1, 0.0, pltpu.roll(x, n - 1, 0))


def tap_sums(g):
    ends = g[0] + g[2]
    return [g[0], ends + g[1], ends - g[1], g[2]]


def pair_outputs(m):
    return m[0] + 0.5 * (m[1] + m[2]), 0.5 * (m[1] - m[2]) - m[3]


def exchange_kernel(
    sizes, lat_hbm, wm_hbm, w1_hbm, z_ref, u_ref, w1_ref,
    got, lat_ref, pad_a, pad_b, packed, stage, raw, main, tail, rowtap,
    send_sem, recv_sem, own_sem, lat_sem, wm_sem, w1_sem,
):
    tiles, strips, frames, shard_rows = sizes
    quarters = tiles // frames
    blocks = tiles // strips
    offset = strips // 2 - 1
    me = lax.axis_index("tile")
    fetch = pltpu.make_async_copy(lat_hbm, lat_ref, lat_sem)
    fetch.start()
    ch = raw.shape[-1]
    group = w1_hbm.shape[1] // 3
    weights = [pltpu.make_async_copy(wm_hbm.at[dt], raw.at[dt], wm_sem.at[dt]) for dt in range(3)]
    inputs = [
        pltpu.make_async_copy(
            w1_hbm.at[dt, pl.ds(dr * group, group)],
            w1_ref.at[dt, pl.ds(dr * GAP, group)],
            w1_sem.at[3 * dt + dr],
        )
        for dt in range(3)
        for dr in range(3)
    ]
    for copy in weights + inputs:
        copy.start(priority=1)
    barrier = pltpu.get_barrier_semaphore()
    for step in range(1, tiles):
        pl.semaphore_signal(barrier, inc=1, device_id={"tile": lax.rem(me + step, tiles)})

    wl = lat_ref.shape[1]
    fetch.wait()
    values = lat_ref[...].astype(jnp.float32)
    spare = jnp.zeros((2 * LANES - values.shape[0], wl), jnp.float32)
    for pad, rows in ((pad_a, values[:LANES]), (pad_b, jnp.concatenate([values[LANES:], spare]))):
        pad[:8] = jnp.zeros((8, LANES), jnp.float32)
        pad[8 + wl :] = jnp.zeros((WS, LANES), jnp.float32)
        pad[8 : 8 + wl] = rows.T
    low = lax.broadcasted_iota(jnp.int32, (HALF, LANES), 1) < LANES // 2
    for s in range(strips):
        at = WS * s + 8 - 3
        packed[s, :WIDE] = pad_a[at : at + WIDE]
        upper = pltpu.roll(pad_b[at + HALF : at + 2 * HALF], LANES // 2, 1)
        packed[s, WIDE:] = jnp.where(low, pad_b[at : at + HALF], upper)
        stage[s] = packed[s].astype(jnp.bfloat16)
    pl.semaphore_wait(barrier, tiles - 1)

    frame = me // quarters
    quarter = me % quarters

    def each_send(act):
        for ahead in range(3):
            block = frame // TF + ahead
            slot = (2 * TF - TF * ahead + frame % TF) * quarters + quarter

            @pl.when(block < blocks)
            def _():
                @pl.loop(0, strips)
                def _(j):
                    s = (j + me) % strips
                    to = (block * strips + s + offset) % tiles

                    @pl.when(to != me)
                    def _():
                        act(
                            pltpu.make_async_remote_copy(
                                src_ref=stage.at[s],
                                dst_ref=got.at[slot],
                                send_sem=send_sem.at[ahead * strips + s],
                                recv_sem=recv_sem.at[slot],
                                device_id={"tile": to},
                            ),
                            None,
                        )

                    @pl.when(to == me)
                    def _():
                        act(None, pltpu.make_async_copy(stage.at[s], got.at[slot], own_sem))

    def start(remote, local):
        (remote if local is None else local).start()

    def finish(remote, local):
        if local is None:
            remote.wait_send()

    each_send(start)

    for dt in range(3):
        for dr in range(3):
            end = (dr + 1) * GAP if dr < 2 else w1_ref.shape[1]
            w1_ref[dt, dr * GAP + group : end] = jnp.zeros((end - dr * GAP - group, ch), jnp.bfloat16)
    for dt in range(3):
        weights[dt].wait()

        @pl.loop(0, ch // CHUNK)
        def _(step, dt=dt):
            rows = pl.ds(pl.multiple_of(step * CHUNK, CHUNK), CHUNK)
            for at in range(0, ch, LANES):
                cols = pl.ds(at, LANES)
                across = [
                    tap_sums([raw[dt, dr, dc, rows, cols].astype(jnp.float32) for dr in range(3)])
                    for dc in range(3)
                ]
                for i in range(4):
                    for j, value in enumerate(tap_sums([across[dc][i] for dc in range(3)])):
                        u_ref[4 * i + j, dt, rows, cols] = value.astype(jnp.bfloat16)

    for copy in inputs:
        copy.wait()
    mine = (me + tiles - offset) % tiles // strips
    hl = quarters * shard_rows
    hh = hl // 2
    aw = WS + 3
    clat = group // 3
    per = LANES // clat
    wide = rowtap.shape[0] // (hl + 2)
    rowtap[:wide] = jnp.zeros((wide, LANES), jnp.float32)
    rowtap[(hl + 1) * wide :] = jnp.zeros((wide, LANES), jnp.float32)
    at_lane = lax.broadcasted_iota(jnp.int32, (wide, LANES), 1)

    @pl.loop(0, 3 * TF)
    def _(step):
        f = jnp.where(frame >= TF * mine, 3 * TF - 1 - step, step)
        begin = (TF * mine - 2 * TF + f) * quarters

        @pl.when(begin >= 0)
        def _():
            @pl.loop(0, quarters)
            def _(q):
                slot = f * quarters + q

                @pl.when(begin + q != me)
                def _():
                    pltpu.make_async_remote_copy(
                        src_ref=stage.at[0],
                        dst_ref=got.at[slot],
                        send_sem=send_sem.at[0],
                        recv_sem=recv_sem.at[slot],
                        device_id={"tile": me},
                    ).wait_recv()

                @pl.when(begin + q == me)
                def _():
                    pltpu.make_async_copy(stage.at[0], got.at[slot], own_sem).wait()

                main[...] = got[slot].astype(jnp.float32)
                tail[:HALF] = main[WIDE:]
                tail[HALF : 2 * HALF] = pltpu.roll(main[WIDE:], LANES // 2, 1)
                for first_row, count, x in ((0, per, main), (per, shard_rows - per, tail)):
                    shifts = [x[dc : dc + wide] for dc in range(3)]
                    for r in range(count):
                        y = jnp.zeros((wide, LANES), jnp.float32)
                        for dc in (2, 1, 0):
                            turn = (dc - r) * clat % LANES
                            moved = pltpu.roll(shifts[dc], turn, 1) if turn else shifts[dc]
                            y = jnp.where(at_lane < (dc + 1) * clat, moved, y)
                        start = pl.multiple_of((1 + q * shard_rows + first_row + r) * wide, 8)
                        rowtap[pl.ds(start, wide)] = y

            for w in range(aw):
                v = [rowtap[pl.ds(k * wide + w, hh, stride=2 * wide), :] for k in range(4)]
                turned = [pltpu.roll(v[k], GAP, 1) for k in (1, 2)]
                low = jnp.concatenate([v[0] + turned[0], v[1] + turned[1]])
                z_ref[f, w, :, :LANES] = low.astype(jnp.bfloat16)
                z_ref[f, w, :, LANES:] = jnp.concatenate(v[2:]).astype(jnp.bfloat16)

    each_send(finish)


def decode_kernel(
    sizes, clip, z_ref, w1_ref, g1_ref, u_ref, g2_ref, hw_ref, out_ref,
    v_ref, v3_ref, va_ref, vb_ref, r_ref, firstb, fscr, ya_ref, yb_ref, outw, head_ref,
):
    tiles, strips, hl, clat, shard_rows = sizes
    ch = g1_ref.shape[-1]
    patch = hw_ref.shape[0] // 3
    half = patch // 2
    aw = WS + 3
    ow = WS + 1
    hh = hl // 2
    lanes = WS * half
    rotated = (lax.axis_index("tile") + tiles - (strips // 2 - 1)) % tiles
    strip = rotated % strips
    block = rotated // strips

    def clip_of(i):
        at = block * TF - 2 * TF + i
        return jnp.where(at < 0, -1, clip[jnp.maximum(at, 0)])

    scal = [clip_of(i) for i in range(3 * TF)]
    g1 = g1_ref[...].reshape(1, ch)
    g2 = g2_ref[...].reshape(1, ch)

    same12 = scal[3] == scal[4]
    same23 = scal[4] == scal[5]
    same02 = scal[2] == scal[4]
    def first_dot(f, keeps, at):
        count = len(keeps)
        taps = [z_ref[f + 3 - count + k].reshape(aw * hl, -1) for k in range(count)]
        taps = [x if keep is None else jnp.where(keep, x, 0) for x, keep in zip(taps, keeps)]
        fscr[at] = jnp.dot(
            jnp.concatenate(taps, axis=-1), w1_ref[3 - count :].reshape(-1, ch),
            preferred_element_type=jnp.float32,
        ).reshape(aw, hl, ch)

    def first_norm(f, w, at, inside):
        rounded = fscr[at, w].astype(jnp.bfloat16)
        if not isinstance(f, int):
            firstb[jnp.maximum(f - 2, 0), w] = rounded
        elif f >= 2:
            firstb[f - 2, w] = rounded
        value = norm_act(rounded.astype(jnp.float32), g1)
        if inside is not None:
            value = value * inside.astype(jnp.float32)
        even, odd = value[:hh], value[hh:]
        r_ref[f, w, 0] = row_shift(odd, 1) - odd
        r_ref[f, w, 1] = even + odd
        r_ref[f, w, 2] = odd - even
        r_ref[f, w, 3] = even - row_shift(even, -1)

    def first(f, *keeps):
        first_dot(f, keeps, f % 2)
        for w in range(aw):
            first_norm(f, w, f % 2, strip > 0 if w < 2 else strip < strips - 1 if w == aw - 1 else None)

    def expand(f, i, dst):
        for c in range(0, PAIRS, 2):
            d = [r_ref[f, 2 * c + k, i] for k in range(min(6, aw - 2 * c))]
            cells = [[d[0] - d[2], d[1] + d[2], d[2] - d[1], d[1] - d[3] if len(d) > 3 else d[1]]]
            if c + 1 < PAIRS:
                cells.append([d[2] - d[4], d[3] + d[4], d[4] - d[3], d[3] - d[5]])
            else:
                cells.append([jnp.zeros((8, ch), jnp.float32)] * 4)
            for j in range(4):
                both = jnp.concatenate([cell[j] for cell in cells])
                dst[j, c * hh : c * hh + both.shape[0]] = both.astype(jnp.bfloat16)

    def product(sides, weights):
        return jnp.dot(
            jnp.concatenate(sides, axis=-1), jnp.concatenate(weights, axis=0),
            preferred_element_type=jnp.float32,
        )

    def product_both(sides, comp):
        w0, w1, w2 = [u_ref[comp, dt] for dt in range(3)]
        return product(
            sides, [jnp.concatenate([w1, w0], axis=-1), jnp.concatenate([w2, w1], axis=-1)]
        )

    def put(y, i, sums):
        y[i, 0], y[i, 1] = pair_outputs(sums)

    def put_more(y, i, sums):
        front, back = pair_outputs(sums)
        y[i, 0] += front
        y[i, 1] += back

    rows = lax.broadcasted_iota(jnp.int32, (3 * patch, 6 * lanes), 0)
    cols = lax.broadcasted_iota(jnp.int32, (3 * patch, 6 * lanes), 1)
    odd = cols // (3 * lanes)
    colour = (cols // lanes) % 3
    want = colour * patch + (cols % lanes + half * odd) % patch
    spread = (rows == want).astype(jnp.bfloat16)
    head_ref[...] = lax.dot_general(
        hw_ref[...], spread, (((0,), (0,)), ((), ())), preferred_element_type=jnp.float32
    ).astype(jnp.bfloat16)
    lane = lax.broadcasted_iota(jnp.int32, (hl, lanes), 1)

    def outward(fo, y, cell, side):
        part = pl.ds(pl.multiple_of(cell * hh, 8), hh)
        added = jnp.concatenate(pair_outputs([y[i, side, part] for i in range(4)]))
        value = norm_act(firstb[fo, 2 * cell + side + 1].astype(jnp.float32) + added, g2)
        if side == 0:
            value = value * jnp.logical_or(cell > 0, strip > 0).astype(jnp.float32)
        outw[side, cell] = value.astype(jnp.bfloat16)

    def picture(fo):
        p_odd = jnp.dot(
            outw[0].reshape(-1, ch), head_ref[:, 3 * lanes :], preferred_element_type=jnp.float32
        )
        p_even = jnp.dot(
            outw[1, : WS // 2].reshape(-1, ch), head_ref[:, : 3 * lanes],
            preferred_element_type=jnp.float32,
        )
        for k in range(3):
            front = jnp.zeros((hl, lanes), jnp.float32)
            back = jnp.zeros((hl, lanes), jnp.float32)
            for i in range(WS // 2):
                piece = p_even[i * hl : (i + 1) * hl, k * lanes : (k + 1) * lanes]
                front = jnp.where(lane // patch == i, piece, front)
            for i in range(WS // 2 + 1):
                piece = p_odd[i * hl : (i + 1) * hl, k * lanes : (k + 1) * lanes]
                back = jnp.where((lane + half) // patch == i, piece, back)
            out_ref[fo, k, pl.ds(0, hh, stride=2), :] = (front + back)[:hh]
            out_ref[fo, k, pl.ds(1, hh, stride=2), :] = (front + back)[hh:]

    late = jnp.logical_not(same02)
    early = jnp.logical_and(jnp.logical_and(same02, jnp.logical_not(same23)), scal[1] != scal[2])

    def all_outward(fo, y):
        for w in range(ow):
            outward(fo, y, w // 2, w % 2)
        picture(fo)

    def halves(body):
        @pl.loop(0, 2)
        def _(pair):
            body(2 * pair, va_ref, vb_ref)
            body(2 * pair + 1, vb_ref, va_ref)

    def quarters_of(body):
        for pair in range(2):
            body(2 * pair, va_ref, vb_ref)
            body(2 * pair + 1, vb_ref, va_ref)

    @pl.when(late)
    def _():
        @pl.when(same12)
        def _():
            first(1, None)

        @pl.when(jnp.logical_not(same12))
        def _():
            r_ref[1] = jnp.zeros(r_ref.shape[1:], jnp.float32)

        first(2, same12, None)
        expand(1, 0, va_ref.at[0])
        expand(2, 0, va_ref.at[1])
        first(3, scal[3] == scal[5], same23, None)
        use_last = same23.astype(jnp.float32)

        def both(i, now, later):
            after = min(i + 1, 3)
            sums = []
            for j in range(4):
                sums.append(product_both([now[0, j], now[1, j]], 4 * i + j))
                if j in (1, 2):
                    expand(j, after, later.at[j - 1])
                if j == 3:
                    expand(3, i, v3_ref.at[pl.ds(4 * i, 4)])
            put(ya_ref, i, [x[:, :ch] for x in sums])
            put(yb_ref, i, [use_last * x[:, ch:] for x in sums])

        def last(i, now, later):
            sums = [product([v3_ref[4 * i + j]], [u_ref[4 * i + j, 2]]) for j in range(4)]
            for k in range(4):
                outward(0, ya_ref, 2 * i + k // 2, k % 2)
            put_more(yb_ref, i, sums)

        quarters_of(both)
        quarters_of(last)
        outward(0, ya_ref, WS // 2, 0)
        picture(0)

    @pl.when(early)
    def _():
        first(3, None)
        first(2, None, None, None)
        for i in range(4):
            expand(3, i, v3_ref.at[pl.ds(4 * i, 4)])
        first(1, None, None)
        first(0, None)

        def alone(i, now, later):
            sums = []
            for j in range(4):
                sums.append(product([v3_ref[4 * i + j]], [u_ref[4 * i + j, 2]]))
                if j < 3:
                    expand(j, i, v_ref.at[j, pl.ds(4 * i, 4)])
            put(ya_ref, i, sums)

        def three(i, now, later):
            sums = [
                product(
                    [v_ref[f, 4 * i + j] for f in range(3)], [u_ref[4 * i + j, dt] for dt in range(3)]
                )
                for j in range(4)
            ]
            for k in range(4):
                outward(1, ya_ref, 2 * i + k // 2, k % 2)
            put(yb_ref, i, sums)

        quarters_of(alone)
        quarters_of(three)
        outward(1, ya_ref, WS // 2, 0)
        picture(1)

    @pl.when(jnp.logical_not(jnp.logical_or(late, early)))
    def _():
        ya_ref[...] = jnp.zeros_like(ya_ref)
        yb_ref[...] = jnp.zeros_like(yb_ref)

        @pl.loop(0, TF + 2)
        def _(f):
            ids = [clip_of(f + dt) for dt in range(3)]
            first_dot(f, [ids[0] == ids[2], ids[1] == ids[2], None], 0)

            @pl.loop(0, aw)
            def _(w):
                first_norm(f, w, 0, ((strip > 0) | (w >= 2)) & ((strip < strips - 1) | (w < aw - 1)))

            @pl.loop(0, 4)
            def _(i):
                expand(f, i, v3_ref.at[pl.ds(4 * i, 4)])

            for fo, y in enumerate((ya_ref, yb_ref)):

                @pl.when(jnp.logical_and(jnp.logical_and(f >= fo, f <= fo + 2), ids[2] == scal[4 + fo]))
                def _(fo=fo, y=y):
                    @pl.loop(0, 4)
                    def _(i):
                        @pl.loop(0, 4)
                        def _(j):
                            one = product([v3_ref[4 * i + j]], [u_ref[4 * i + j, f - fo]])
                            y[i, 0] += jnp.where(j == 0, 1.0, jnp.where(j == 3, 0.0, 0.5)) * one
                            y[i, 1] += jnp.where(j == 0, 0.0, jnp.where(j == 3, -1.0, 1.5 - j)) * one

        all_outward(0, ya_ref)

    all_outward(jnp.where(early, 0, 1), yb_ref)


def decode_call(sizes, patch, ch, operands):
    tiles, strips, hl, clat, shard_rows = sizes
    aw = WS + 3
    half = patch // 2
    mrows = -(-PAIRS * (hl // 2) // 16) * 16
    vm = pl.BlockSpec(memory_space=pltpu.VMEM)
    return pl.pallas_call(
        functools.partial(decode_kernel, sizes),
        out_shape=jax.ShapeDtypeStruct((TF, 3, hl, WS * half), jnp.float32),
        in_specs=[pl.BlockSpec(memory_space=pltpu.SMEM)] + [vm] * 6,
        out_specs=vm,
        scratch_shapes=[
            pltpu.VMEM((TF + 1, 16, mrows, ch), jnp.bfloat16),
            pltpu.VMEM((16, mrows, ch), jnp.bfloat16),
            pltpu.VMEM((2, 4, mrows, ch), jnp.bfloat16),
            pltpu.VMEM((2, 4, mrows, ch), jnp.bfloat16),
            pltpu.VMEM((TF + 2, aw, 4, hl // 2, ch), jnp.float32),
            pltpu.VMEM((TF, aw, hl, ch), jnp.bfloat16),
            pltpu.VMEM((2, aw, hl, ch), jnp.float32),
            pltpu.VMEM((4, 2, mrows, ch), jnp.float32),
            pltpu.VMEM((4, 2, mrows, ch), jnp.float32),
            pltpu.VMEM((2, WS // 2 + 1, hl, ch), jnp.bfloat16),
            pltpu.VMEM((ch, 6 * WS * half), jnp.bfloat16),
        ],
        compiler_params=pltpu.CompilerParams(vmem_limit_bytes=40 * 1024 * 1024),
    )(*operands)


def per_device(latents, clip_index, first_conv, first_gain, middle_conv, head_gain, head_weight):
    tiles = lax.axis_size("tile")
    shard_rows, clat, wl = latents.shape
    ch = first_gain.shape[0]
    frames = clip_index.shape[0]
    hl = tiles * shard_rows // frames
    strips = wl // WS
    quarters = tiles // frames
    slots = 3 * TF * quarters
    vm = pl.BlockSpec(memory_space=pltpu.VMEM)
    fields, sums, first_taps = pl.pallas_call(
        functools.partial(exchange_kernel, (tiles, strips, frames, shard_rows)),
        out_shape=[
            pltpu.VMEM((3 * TF, WS + 3, hl, 2 * LANES), jnp.bfloat16),
            pltpu.VMEM((16, 3, ch, ch), jnp.bfloat16),
            pltpu.VMEM((3, 2 * LANES, ch), jnp.bfloat16),
        ],
        in_specs=[pl.BlockSpec(memory_space=pl.ANY)] * 3,
        out_specs=[vm] * 3,
        scratch_shapes=[
            pltpu.VMEM((slots, WIDE + HALF, LANES), jnp.bfloat16),
            pltpu.VMEM((shard_rows * clat, wl), jnp.bfloat16),
            pltpu.VMEM((8 + wl + WS, LANES), jnp.float32),
            pltpu.VMEM((8 + wl + WS, LANES), jnp.float32),
            pltpu.VMEM((strips, WIDE + HALF, LANES), jnp.float32),
            pltpu.VMEM((strips, WIDE + HALF, LANES), jnp.bfloat16),
            pltpu.VMEM((3, 3, 3, ch, ch), jnp.bfloat16),
            pltpu.VMEM((WIDE + HALF, LANES), jnp.float32),
            pltpu.VMEM((WIDE + HALF, LANES), jnp.float32),
            pltpu.VMEM(((hl + 2) * 24, LANES), jnp.float32),
            pltpu.SemaphoreType.DMA((3 * strips,)),
            pltpu.SemaphoreType.DMA((slots,)),
            pltpu.SemaphoreType.DMA,
            pltpu.SemaphoreType.DMA,
            pltpu.SemaphoreType.DMA((3,)),
            pltpu.SemaphoreType.DMA((9,)),
        ],
        compiler_params=pltpu.CompilerParams(
            collective_id=0, has_side_effects=True, vmem_limit_bytes=40 * 1024 * 1024
        ),
    )(*[
        pltpu.with_memory_space_constraint(x, pltpu.HBM)
        for x in (latents.reshape(shard_rows * clat, wl), middle_conv, first_conv.reshape(3, 9 * clat, ch))
    ])
    fields, sums, first_taps = [
        pltpu.with_memory_space_constraint(x, pltpu.VMEM) for x in (fields, sums, first_taps)
    ]
    out = decode_call(
        (tiles, strips, hl, clat, shard_rows), head_weight.shape[1] // 3, ch,
        (clip_index, fields, first_taps, first_gain, sums, head_gain, head_weight.T),
    )
    return out[None]


def solution(mesh):
    placed = (P(("group", "tile"), None, None), P("group"), P(), P(), P(), P(), P())
    return jax.shard_map(
        per_device,
        mesh=mesh,
        in_specs=placed,
        out_specs=P(("group", "tile"), None, None, None, None),
        check_vma=False,
    )
```

```python
import functools

import jax
import jax.numpy as jnp
from jax import lax
from jax.experimental import pallas as pl
from jax.experimental.pallas import tpu as pltpu
from jax.sharding import PartitionSpec as P

WS = 16
TF = 2
LANES = 128
GAP = LANES // 2
WIDE = WS + 5
HALF = (WIDE + 1) // 2
PAIRS = (WS + 2) // 2
CHUNK = 16


def norm_act(x, gain):
    scale = lax.rsqrt(jnp.mean(x * x, axis=-1, keepdims=True) + 1e-06)
    h = x * scale * (0.5 * gain)
    return h + h * jnp.tanh(h)


def row_shift(x, by):
    rows = lax.broadcasted_iota(jnp.int32, x.shape, 0)
    n = x.shape[0]
    if by > 0:
        return jnp.where(rows == 0, 0.0, pltpu.roll(x, 1, 0))
    return jnp.where(rows == n - 1, 0.0, pltpu.roll(x, n - 1, 0))


def tap_sums(g):
    ends = g[0] + g[2]
    return [g[0], ends + g[1], ends - g[1], g[2]]


def pair_outputs(m):
    return m[0] + 0.5 * (m[1] + m[2]), 0.5 * (m[1] - m[2]) - m[3]


def exchange_kernel(
    sizes, lat_hbm, wm_hbm, w1_hbm, z_ref, u_ref, w1_ref,
    got, lat_ref, pad_a, pad_b, packed, stage, raw, main, tail, rowtap,
    send_sem, recv_sem, own_sem, lat_sem, wm_sem, w1_sem,
):
    tiles, strips, frames, shard_rows = sizes
    quarters = tiles // frames
    blocks = tiles // strips
    offset = strips // 2 - 1
    me = lax.axis_index("tile")
    fetch = pltpu.make_async_copy(lat_hbm, lat_ref, lat_sem)
    fetch.start()
    ch = raw.shape[-1]
    group = w1_hbm.shape[1] // 3
    weights = [pltpu.make_async_copy(wm_hbm.at[dt], raw.at[dt], wm_sem.at[dt]) for dt in range(3)]
    inputs = [
        pltpu.make_async_copy(
            w1_hbm.at[dt, pl.ds(dr * group, group)],
            w1_ref.at[dt, pl.ds(dr * GAP, group)],
            w1_sem.at[3 * dt + dr],
        )
        for dt in range(3)
        for dr in range(3)
    ]
    for copy in weights + inputs:
        copy.start(priority=1)
    barrier = pltpu.get_barrier_semaphore()
    for step in range(1, tiles):
        pl.semaphore_signal(barrier, inc=1, device_id={"tile": lax.rem(me + step, tiles)})

    wl = lat_ref.shape[1]
    fetch.wait()
    values = lat_ref[...].astype(jnp.float32)
    spare = jnp.zeros((2 * LANES - values.shape[0], wl), jnp.float32)
    for pad, rows in ((pad_a, values[:LANES]), (pad_b, jnp.concatenate([values[LANES:], spare]))):
        pad[:8] = jnp.zeros((8, LANES), jnp.float32)
        pad[8 + wl :] = jnp.zeros((WS, LANES), jnp.float32)
        pad[8 : 8 + wl] = rows.T
    low = lax.broadcasted_iota(jnp.int32, (HALF, LANES), 1) < LANES // 2
    for s in range(strips):
        at = WS * s + 8 - 3
        packed[s, :WIDE] = pad_a[at : at + WIDE]
        upper = pltpu.roll(pad_b[at + HALF : at + 2 * HALF], LANES // 2, 1)
        packed[s, WIDE:] = jnp.where(low, pad_b[at : at + HALF], upper)
        stage[s] = packed[s].astype(jnp.bfloat16)
    pl.semaphore_wait(barrier, tiles - 1)

    frame = me // quarters
    quarter = me % quarters

    def each_send(act):
        for ahead in (2, 1, 0):
            block = frame // TF + ahead
            slot = (2 * TF - TF * ahead + frame % TF) * quarters + quarter

            @pl.when(block < blocks)
            def _():
                @pl.loop(0, strips)
                def _(j):
                    s = ((strips // 2 if ahead else strips - 1) + strips - j) % strips
                    to = (block * strips + s + offset) % tiles

                    @pl.when(to != me)
                    def _():
                        act(
                            pltpu.make_async_remote_copy(
                                src_ref=stage.at[s],
                                dst_ref=got.at[slot],
                                send_sem=send_sem.at[ahead * strips + s],
                                recv_sem=recv_sem.at[slot],
                                device_id={"tile": to},
                            ),
                            None,
                        )

                    @pl.when(to == me)
                    def _():
                        act(None, pltpu.make_async_copy(stage.at[s], got.at[slot], own_sem))

    def start(remote, local):
        (remote if local is None else local).start()

    def finish(remote, local):
        if local is None:
            remote.wait_send()

    each_send(start)

    for dt in range(3):
        for dr in range(3):
            end = (dr + 1) * GAP if dr < 2 else w1_ref.shape[1]
            w1_ref[dt, dr * GAP + group : end] = jnp.zeros((end - dr * GAP - group, ch), jnp.bfloat16)
    for dt in range(3):
        weights[dt].wait()

        @pl.loop(0, ch // CHUNK)
        def _(step, dt=dt):
            rows = pl.ds(pl.multiple_of(step * CHUNK, CHUNK), CHUNK)
            for at in range(0, ch, LANES):
                cols = pl.ds(at, LANES)
                across = [
                    tap_sums([raw[dt, dr, dc, rows, cols].astype(jnp.float32) for dr in range(3)])
                    for dc in range(3)
                ]
                for i in range(4):
                    for j, value in enumerate(tap_sums([across[dc][i] for dc in range(3)])):
                        u_ref[4 * i + j, dt, rows, cols] = value.astype(jnp.bfloat16)

    for copy in inputs:
        copy.wait()
    mine = (me + tiles - offset) % tiles // strips
    hl = quarters * shard_rows
    hh = hl // 2
    aw = WS + 3
    clat = group // 3
    per = LANES // clat
    wide = rowtap.shape[0] // (hl + 2)
    rowtap[:wide] = jnp.zeros((wide, LANES), jnp.float32)
    rowtap[(hl + 1) * wide :] = jnp.zeros((wide, LANES), jnp.float32)
    at_lane = lax.broadcasted_iota(jnp.int32, (wide, LANES), 1)

    @pl.loop(0, 3 * TF)
    def _(step):
        f = jnp.where(frame >= TF * mine, 3 * TF - 1 - step, step)
        begin = (TF * mine - 2 * TF + f) * quarters

        @pl.when(begin >= 0)
        def _():
            @pl.loop(0, quarters)
            def _(q):
                slot = f * quarters + q

                @pl.when(begin + q != me)
                def _():
                    pltpu.make_async_remote_copy(
                        src_ref=stage.at[0],
                        dst_ref=got.at[slot],
                        send_sem=send_sem.at[0],
                        recv_sem=recv_sem.at[slot],
                        device_id={"tile": me},
                    ).wait_recv()

                @pl.when(begin + q == me)
                def _():
                    pltpu.make_async_copy(stage.at[0], got.at[slot], own_sem).wait()

            for q in range(quarters):
                main[q] = got[f * quarters + q].astype(jnp.float32)
                tail[q, :HALF] = main[q, WIDE:]
                tail[q, HALF : 2 * HALF] = pltpu.roll(main[q, WIDE:], LANES // 2, 1)
                for first_row, count, x in ((0, per, main.at[q]), (per, shard_rows - per, tail.at[q])):
                    shifts = [x[dc : dc + wide] for dc in range(3)]
                    for r in range(count):
                        y = jnp.zeros((wide, LANES), jnp.float32)
                        for dc in (2, 1, 0):
                            turn = (dc - r) * clat % LANES
                            moved = pltpu.roll(shifts[dc], turn, 1) if turn else shifts[dc]
                            y = jnp.where(at_lane < (dc + 1) * clat, moved, y)
                        start = (1 + q * shard_rows + first_row + r) * wide
                        rowtap[start : start + wide] = y

            for w in range(aw):
                v = [rowtap[pl.ds(k * wide + w, hh, stride=2 * wide), :] for k in range(4)]
                turned = [pltpu.roll(v[k], GAP, 1) for k in (1, 2)]
                low = jnp.concatenate([v[0] + turned[0], v[1] + turned[1]])
                z_ref[f, w, :, :LANES] = low.astype(jnp.bfloat16)
                z_ref[f, w, :, LANES:] = jnp.concatenate(v[2:]).astype(jnp.bfloat16)

    each_send(finish)


def decode_kernel(
    sizes, clip, z_ref, w1_ref, g1_ref, u_ref, g2_ref, hw_ref, out_ref,
    v_ref, v3_ref, va_ref, vb_ref, r_ref, firstb, fscr, ya_ref, yb_ref, outw, head_ref,
):
    tiles, strips, hl, clat, shard_rows = sizes
    ch = g1_ref.shape[-1]
    patch = hw_ref.shape[0] // 3
    half = patch // 2
    aw = WS + 3
    ow = WS + 1
    hh = hl // 2
    lanes = WS * half
    rotated = (lax.axis_index("tile") + tiles - (strips // 2 - 1)) % tiles
    strip = rotated % strips
    block = rotated // strips

    def clip_of(i):
        at = block * TF - 2 * TF + i
        return jnp.where(at < 0, -1, clip[jnp.maximum(at, 0)])

    scal = [clip_of(i) for i in range(3 * TF)]
    g1 = g1_ref[...].reshape(1, ch)
    g2 = g2_ref[...].reshape(1, ch)

    same12 = scal[3] == scal[4]
    same23 = scal[4] == scal[5]
    same02 = scal[2] == scal[4]
    def first_dot(f, keeps, at):
        count = len(keeps)
        taps = [z_ref[f + 3 - count + k].reshape(aw * hl, -1) for k in range(count)]
        taps = [x if keep is None else jnp.where(keep, x, 0) for x, keep in zip(taps, keeps)]
        fscr[at] = jnp.dot(
            jnp.concatenate(taps, axis=-1), w1_ref[3 - count :].reshape(-1, ch),
            preferred_element_type=jnp.float32,
        ).reshape(aw, hl, ch)

    def first_norm(f, w, at, inside):
        rounded = fscr[at, w].astype(jnp.bfloat16)
        if not isinstance(f, int):
            firstb[jnp.maximum(f - 2, 0), w] = rounded
        elif f >= 2:
            firstb[f - 2, w] = rounded
        value = norm_act(rounded.astype(jnp.float32), g1)
        if inside is not None:
            value = value * inside.astype(jnp.float32)
        even, odd = value[:hh], value[hh:]
        r_ref[f, w, 0] = row_shift(odd, 1) - odd
        r_ref[f, w, 1] = even + odd
        r_ref[f, w, 2] = odd - even
        r_ref[f, w, 3] = even - row_shift(even, -1)

    def first(f, *keeps):
        first_dot(f, keeps, f % 2)
        for w in range(aw):
            first_norm(f, w, f % 2, strip > 0 if w < 2 else strip < strips - 1 if w == aw - 1 else None)

    def expand(f, i, dst):
        for c in range(0, PAIRS, 2):
            d = [r_ref[f, 2 * c + k, i] for k in range(min(6, aw - 2 * c))]
            cells = [[d[0] - d[2], d[1] + d[2], d[2] - d[1], d[1] - d[3] if len(d) > 3 else d[1]]]
            if c + 1 < PAIRS:
                cells.append([d[2] - d[4], d[3] + d[4], d[4] - d[3], d[3] - d[5]])
            else:
                cells.append([jnp.zeros((8, ch), jnp.float32)] * 4)
            for j in range(4):
                both = jnp.concatenate([cell[j] for cell in cells])
                dst[j, c * hh : c * hh + both.shape[0]] = both.astype(jnp.bfloat16)

    def product(sides, weights):
        return jnp.dot(
            jnp.concatenate(sides, axis=-1), jnp.concatenate(weights, axis=0),
            preferred_element_type=jnp.float32,
        )

    def product_both(sides, comp):
        w0, w1, w2 = [u_ref[comp, dt] for dt in range(3)]
        return product(
            sides, [jnp.concatenate([w1, w0], axis=-1), jnp.concatenate([w2, w1], axis=-1)]
        )

    def put(y, i, sums):
        y[i, 0], y[i, 1] = pair_outputs(sums)

    def put_more(y, i, sums):
        front, back = pair_outputs(sums)
        y[i, 0] += front
        y[i, 1] += back

    rows = lax.broadcasted_iota(jnp.int32, (3 * patch, 6 * lanes), 0)
    cols = lax.broadcasted_iota(jnp.int32, (3 * patch, 6 * lanes), 1)
    odd = cols // (3 * lanes)
    colour = (cols // lanes) % 3
    want = colour * patch + (cols % lanes + half * odd) % patch
    spread = (rows == want).astype(jnp.bfloat16)
    head_ref[...] = lax.dot_general(
        hw_ref[...], spread, (((0,), (0,)), ((), ())), preferred_element_type=jnp.float32
    ).astype(jnp.bfloat16)
    lane = lax.broadcasted_iota(jnp.int32, (hl, lanes), 1)

    def outward(fo, y, cell, side):
        part = pl.ds(pl.multiple_of(cell * hh, 8), hh)
        added = jnp.concatenate(pair_outputs([y[i, side, part] for i in range(4)]))
        value = norm_act(firstb[fo, 2 * cell + side + 1].astype(jnp.float32) + added, g2)
        if side == 0:
            value = value * jnp.logical_or(cell > 0, strip > 0).astype(jnp.float32)
        outw[side, cell] = value.astype(jnp.bfloat16)

    def picture(fo):
        p_odd = jnp.dot(
            outw[0].reshape(-1, ch), head_ref[:, 3 * lanes :], preferred_element_type=jnp.float32
        )
        p_even = jnp.dot(
            outw[1, : WS // 2].reshape(-1, ch), head_ref[:, : 3 * lanes],
            preferred_element_type=jnp.float32,
        )
        for k in range(3):
            front = jnp.zeros((hl, lanes), jnp.float32)
            back = jnp.zeros((hl, lanes), jnp.float32)
            for i in range(WS // 2):
                piece = p_even[i * hl : (i + 1) * hl, k * lanes : (k + 1) * lanes]
                front = jnp.where(lane // patch == i, piece, front)
            for i in range(WS // 2 + 1):
                piece = p_odd[i * hl : (i + 1) * hl, k * lanes : (k + 1) * lanes]
                back = jnp.where((lane + half) // patch == i, piece, back)
            out_ref[fo, k, pl.ds(0, hh, stride=2), :] = (front + back)[:hh]
            out_ref[fo, k, pl.ds(1, hh, stride=2), :] = (front + back)[hh:]

    late = jnp.logical_not(same02)
    early = jnp.logical_and(jnp.logical_and(same02, jnp.logical_not(same23)), scal[1] != scal[2])

    def all_outward(fo, y):
        for w in range(ow):
            outward(fo, y, w // 2, w % 2)
        picture(fo)

    def halves(body):
        @pl.loop(0, 2)
        def _(pair):
            body(2 * pair, va_ref, vb_ref)
            body(2 * pair + 1, vb_ref, va_ref)

    def quarters_of(body):
        for pair in range(2):
            body(2 * pair, va_ref, vb_ref)
            body(2 * pair + 1, vb_ref, va_ref)

    @pl.when(late)
    def _():
        @pl.when(same12)
        def _():
            first(1, None)

        @pl.when(jnp.logical_not(same12))
        def _():
            r_ref[1] = jnp.zeros(r_ref.shape[1:], jnp.float32)

        first(2, same12, None)
        expand(1, 0, va_ref.at[0])
        expand(2, 0, va_ref.at[1])
        first(3, scal[3] == scal[5], same23, None)
        use_last = same23.astype(jnp.float32)

        def both(i, now, later):
            after = min(i + 1, 3)
            sums = []
            for j in range(4):
                sums.append(product_both([now[0, j], now[1, j]], 4 * i + j))
                if j in (1, 2):
                    expand(j, after, later.at[j - 1])
                if j == 3:
                    expand(3, i, v3_ref.at[pl.ds(4 * i, 4)])
            put(ya_ref, i, [x[:, :ch] for x in sums])
            put(yb_ref, i, [use_last * x[:, ch:] for x in sums])

        def last(i, now, later):
            sums = [product([v3_ref[4 * i + j]], [u_ref[4 * i + j, 2]]) for j in range(4)]
            for k in range(4):
                outward(0, ya_ref, 2 * i + k // 2, k % 2)
            put_more(yb_ref, i, sums)

        quarters_of(both)
        quarters_of(last)
        outward(0, ya_ref, WS // 2, 0)
        picture(0)

    @pl.when(early)
    def _():
        first(3, None)
        first(2, None, None, None)
        for i in range(4):
            expand(3, i, v3_ref.at[pl.ds(4 * i, 4)])
        first(1, None, None)
        first(0, None)

        def alone(i, now, later):
            sums = []
            for j in range(4):
                sums.append(product([v3_ref[4 * i + j]], [u_ref[4 * i + j, 2]]))
                if j < 3:
                    expand(j, i, v_ref.at[j, pl.ds(4 * i, 4)])
            put(ya_ref, i, sums)

        def three(i, now, later):
            sums = [
                product(
                    [v_ref[f, 4 * i + j] for f in range(3)], [u_ref[4 * i + j, dt] for dt in range(3)]
                )
                for j in range(4)
            ]
            for k in range(4):
                outward(1, ya_ref, 2 * i + k // 2, k % 2)
            put(yb_ref, i, sums)

        quarters_of(alone)
        quarters_of(three)
        outward(1, ya_ref, WS // 2, 0)
        picture(1)

    @pl.when(jnp.logical_not(jnp.logical_or(late, early)))
    def _():
        ya_ref[...] = jnp.zeros_like(ya_ref)
        yb_ref[...] = jnp.zeros_like(yb_ref)

        @pl.loop(0, TF + 2)
        def _(f):
            ids = [clip_of(f + dt) for dt in range(3)]
            first_dot(f, [ids[0] == ids[2], ids[1] == ids[2], None], 0)

            @pl.loop(0, aw)
            def _(w):
                first_norm(f, w, 0, ((strip > 0) | (w >= 2)) & ((strip < strips - 1) | (w < aw - 1)))

            @pl.loop(0, 4)
            def _(i):
                expand(f, i, v3_ref.at[pl.ds(4 * i, 4)])

            for fo, y in enumerate((ya_ref, yb_ref)):

                @pl.when(jnp.logical_and(jnp.logical_and(f >= fo, f <= fo + 2), ids[2] == scal[4 + fo]))
                def _(fo=fo, y=y):
                    @pl.loop(0, 4)
                    def _(i):
                        @pl.loop(0, 4)
                        def _(j):
                            one = product([v3_ref[4 * i + j]], [u_ref[4 * i + j, f - fo]])
                            y[i, 0] += jnp.where(j == 0, 1.0, jnp.where(j == 3, 0.0, 0.5)) * one
                            y[i, 1] += jnp.where(j == 0, 0.0, jnp.where(j == 3, -1.0, 1.5 - j)) * one

        all_outward(0, ya_ref)

    all_outward(jnp.where(early, 0, 1), yb_ref)


def decode_call(sizes, patch, ch, operands):
    tiles, strips, hl, clat, shard_rows = sizes
    aw = WS + 3
    half = patch // 2
    mrows = -(-PAIRS * (hl // 2) // 16) * 16
    vm = pl.BlockSpec(memory_space=pltpu.VMEM)
    return pl.pallas_call(
        functools.partial(decode_kernel, sizes),
        out_shape=jax.ShapeDtypeStruct((TF, 3, hl, WS * half), jnp.float32),
        in_specs=[pl.BlockSpec(memory_space=pltpu.SMEM)] + [vm] * 6,
        out_specs=vm,
        scratch_shapes=[
            pltpu.VMEM((TF + 1, 16, mrows, ch), jnp.bfloat16),
            pltpu.VMEM((16, mrows, ch), jnp.bfloat16),
            pltpu.VMEM((2, 4, mrows, ch), jnp.bfloat16),
            pltpu.VMEM((2, 4, mrows, ch), jnp.bfloat16),
            pltpu.VMEM((TF + 2, aw, 4, hl // 2, ch), jnp.float32),
            pltpu.VMEM((TF, aw, hl, ch), jnp.bfloat16),
            pltpu.VMEM((2, aw, hl, ch), jnp.float32),
            pltpu.VMEM((4, 2, mrows, ch), jnp.float32),
            pltpu.VMEM((4, 2, mrows, ch), jnp.float32),
            pltpu.VMEM((2, WS // 2 + 1, hl, ch), jnp.bfloat16),
            pltpu.VMEM((ch, 6 * WS * half), jnp.bfloat16),
        ],
        compiler_params=pltpu.CompilerParams(vmem_limit_bytes=40 * 1024 * 1024),
    )(*operands)


def per_device(latents, clip_index, first_conv, first_gain, middle_conv, head_gain, head_weight):
    tiles = lax.axis_size("tile")
    shard_rows, clat, wl = latents.shape
    ch = first_gain.shape[0]
    frames = clip_index.shape[0]
    hl = tiles * shard_rows // frames
    strips = wl // WS
    quarters = tiles // frames
    slots = 3 * TF * quarters
    vm = pl.BlockSpec(memory_space=pltpu.VMEM)
    fields, sums, first_taps = pl.pallas_call(
        functools.partial(exchange_kernel, (tiles, strips, frames, shard_rows)),
        out_shape=[
            pltpu.VMEM((3 * TF, WS + 3, hl, 2 * LANES), jnp.bfloat16),
            pltpu.VMEM((16, 3, ch, ch), jnp.bfloat16),
            pltpu.VMEM((3, 2 * LANES, ch), jnp.bfloat16),
        ],
        in_specs=[pl.BlockSpec(memory_space=pl.ANY)] * 3,
        out_specs=[vm] * 3,
        scratch_shapes=[
            pltpu.VMEM((slots, WIDE + HALF, LANES), jnp.bfloat16),
            pltpu.VMEM((shard_rows * clat, wl), jnp.bfloat16),
            pltpu.VMEM((8 + wl + WS, LANES), jnp.float32),
            pltpu.VMEM((8 + wl + WS, LANES), jnp.float32),
            pltpu.VMEM((strips, WIDE + HALF, LANES), jnp.float32),
            pltpu.VMEM((strips, WIDE + HALF, LANES), jnp.bfloat16),
            pltpu.VMEM((3, 3, 3, ch, ch), jnp.bfloat16),
            pltpu.VMEM((quarters, WIDE + HALF, LANES), jnp.float32),
            pltpu.VMEM((quarters, WIDE + HALF, LANES), jnp.float32),
            pltpu.VMEM(((hl + 2) * 24, LANES), jnp.float32),
            pltpu.SemaphoreType.DMA((3 * strips,)),
            pltpu.SemaphoreType.DMA((slots,)),
            pltpu.SemaphoreType.DMA,
            pltpu.SemaphoreType.DMA,
            pltpu.SemaphoreType.DMA((3,)),
            pltpu.SemaphoreType.DMA((9,)),
        ],
        compiler_params=pltpu.CompilerParams(
            collective_id=0, has_side_effects=True, vmem_limit_bytes=40 * 1024 * 1024
        ),
    )(*[
        pltpu.with_memory_space_constraint(x, pltpu.HBM)
        for x in (latents.reshape(shard_rows * clat, wl), middle_conv, first_conv.reshape(3, 9 * clat, ch))
    ])
    fields, sums, first_taps = [
        pltpu.with_memory_space_constraint(x, pltpu.VMEM) for x in (fields, sums, first_taps)
    ]
    out = decode_call(
        (tiles, strips, hl, clat, shard_rows), head_weight.shape[1] // 3, ch,
        (clip_index, fields, first_taps, first_gain, sums, head_gain, head_weight.T),
    )
    return out[None]


def solution(mesh):
    placed = (P(("group", "tile"), None, None), P("group"), P(), P(), P(), P(), P())
    return jax.shard_map(
        per_device,
        mesh=mesh,
        in_specs=placed,
        out_specs=P(("group", "tile"), None, None, None, None),
        check_vma=False,
    )
```

```python
import functools

import jax
import jax.numpy as jnp
from jax import lax
from jax.experimental import pallas as pl
from jax.experimental.pallas import tpu as pltpu
from jax.sharding import PartitionSpec as P

WS = 16
TF = 2
LANES = 128
GAP = LANES // 2
WIDE = WS + 5
HALF = (WIDE + 1) // 2
PAIRS = (WS + 2) // 2
CHUNK = 16


def norm_act(x, gain):
    scale = lax.rsqrt(jnp.mean(x * x, axis=-1, keepdims=True) + 1e-06)
    h = x * scale * (0.5 * gain)
    return h + h * jnp.tanh(h)


def row_shift(x, by):
    rows = lax.broadcasted_iota(jnp.int32, x.shape, 0)
    n = x.shape[0]
    if by > 0:
        return jnp.where(rows == 0, 0.0, pltpu.roll(x, 1, 0))
    return jnp.where(rows == n - 1, 0.0, pltpu.roll(x, n - 1, 0))


def tap_sums(g):
    ends = g[0] + g[2]
    return [g[0], ends + g[1], ends - g[1], g[2]]


def pair_outputs(m):
    return m[0] + 0.5 * (m[1] + m[2]), 0.5 * (m[1] - m[2]) - m[3]


def exchange_kernel(
    sizes, lat_hbm, wm_hbm, w1_hbm, z_ref, u_ref, w1_ref,
    got, lat_ref, pad_a, pad_b, packed, stage, raw, main, tail, rowtap,
    send_sem, recv_sem, own_sem, lat_sem, wm_sem, w1_sem,
):
    tiles, strips, frames, shard_rows = sizes
    quarters = tiles // frames
    blocks = tiles // strips
    offset = strips // 2 - 1
    me = lax.axis_index("tile")
    fetch = pltpu.make_async_copy(lat_hbm, lat_ref, lat_sem)
    fetch.start()
    ch = raw.shape[-1]
    group = w1_hbm.shape[1] // 3
    weights = [pltpu.make_async_copy(wm_hbm.at[dt], raw.at[dt], wm_sem.at[dt]) for dt in range(3)]
    inputs = [
        pltpu.make_async_copy(
            w1_hbm.at[dt, pl.ds(dr * group, group)],
            w1_ref.at[dt, pl.ds(dr * GAP, group)],
            w1_sem.at[3 * dt + dr],
        )
        for dt in range(3)
        for dr in range(3)
    ]
    for copy in weights + inputs:
        copy.start(priority=1)
    barrier = pltpu.get_barrier_semaphore()
    for step in range(1, tiles):
        pl.semaphore_signal(barrier, inc=1, device_id={"tile": lax.rem(me + step, tiles)})

    wl = lat_ref.shape[1]
    fetch.wait()
    values = lat_ref[...].astype(jnp.float32)
    spare = jnp.zeros((2 * LANES - values.shape[0], wl), jnp.float32)
    for pad, rows in ((pad_a, values[:LANES]), (pad_b, jnp.concatenate([values[LANES:], spare]))):
        pad[:8] = jnp.zeros((8, LANES), jnp.float32)
        pad[8 + wl :] = jnp.zeros((WS, LANES), jnp.float32)
        pad[8 : 8 + wl] = rows.T
    low = lax.broadcasted_iota(jnp.int32, (HALF, LANES), 1) < LANES // 2
    for s in range(strips):
        at = WS * s + 8 - 3
        packed[s, :WIDE] = pad_a[at : at + WIDE]
        upper = pltpu.roll(pad_b[at + HALF : at + 2 * HALF], LANES // 2, 1)
        packed[s, WIDE:] = jnp.where(low, pad_b[at : at + HALF], upper)
        stage[s] = packed[s].astype(jnp.bfloat16)
    pl.semaphore_wait(barrier, tiles - 1)

    frame = me // quarters
    quarter = me % quarters

    def each_send(act):
        for ahead in (2, 1, 0):
            block = frame // TF + ahead
            slot = (2 * TF - TF * ahead + frame % TF) * quarters + quarter

            @pl.when(block < blocks)
            def _():
                @pl.loop(0, strips)
                def _(j):
                    s = ((strips // 2 if ahead else strips - 1) + strips - j) % strips
                    to = (block * strips + s + offset) % tiles

                    @pl.when(to != me)
                    def _():
                        act(
                            pltpu.make_async_remote_copy(
                                src_ref=stage.at[s],
                                dst_ref=got.at[slot],
                                send_sem=send_sem.at[ahead * strips + s],
                                recv_sem=recv_sem.at[slot],
                                device_id={"tile": to},
                            ),
                            None,
                        )

                    @pl.when(to == me)
                    def _():
                        act(None, pltpu.make_async_copy(stage.at[s], got.at[slot], own_sem))

    def start(remote, local):
        (remote if local is None else local).start()

    def finish(remote, local):
        if local is None:
            remote.wait_send()

    each_send(start)

    for dt in range(3):
        for dr in range(3):
            end = (dr + 1) * GAP if dr < 2 else w1_ref.shape[1]
            w1_ref[dt, dr * GAP + group : end] = jnp.zeros((end - dr * GAP - group, ch), jnp.bfloat16)
    for dt in range(3):
        weights[dt].wait()

        @pl.loop(0, ch // CHUNK)
        def _(step, dt=dt):
            rows = pl.ds(pl.multiple_of(step * CHUNK, CHUNK), CHUNK)
            for at in range(0, ch, LANES):
                cols = pl.ds(at, LANES)
                across = [
                    tap_sums([raw[dt, dr, dc, rows, cols].astype(jnp.float32) for dr in range(3)])
                    for dc in range(3)
                ]
                for i in range(4):
                    for j, value in enumerate(tap_sums([across[dc][i] for dc in range(3)])):
                        u_ref[4 * i + j, dt, rows, cols] = value.astype(jnp.bfloat16)

    for copy in inputs:
        copy.wait()
    mine = (me + tiles - offset) % tiles // strips
    hl = quarters * shard_rows
    hh = hl // 2
    aw = WS + 3
    clat = group // 3
    per = LANES // clat
    wide = -(-WIDE // 8) * 8
    pitch = wide + 1
    span = rowtap.shape[0] // 2

    def row_at(row):
        return row % 2 * span + row // 2 * pitch

    for row in (0, hl + 1):
        rowtap[row_at(row) : row_at(row) + wide] = jnp.zeros((wide, LANES), jnp.float32)
    at_lane = lax.broadcasted_iota(jnp.int32, (wide, LANES), 1)

    @pl.loop(0, 3 * TF)
    def _(step):
        f = jnp.where(frame >= TF * mine, 3 * TF - 1 - step, step)
        begin = (TF * mine - 2 * TF + f) * quarters

        @pl.when(begin >= 0)
        def _():
            @pl.loop(0, quarters)
            def _(q):
                slot = f * quarters + q

                @pl.when(begin + q != me)
                def _():
                    pltpu.make_async_remote_copy(
                        src_ref=stage.at[0],
                        dst_ref=got.at[slot],
                        send_sem=send_sem.at[0],
                        recv_sem=recv_sem.at[slot],
                        device_id={"tile": me},
                    ).wait_recv()

                @pl.when(begin + q == me)
                def _():
                    pltpu.make_async_copy(stage.at[0], got.at[slot], own_sem).wait()

            for q in range(quarters):
                main[q] = got[f * quarters + q].astype(jnp.float32)
                tail[q, :HALF] = main[q, WIDE:]
                tail[q, HALF : 2 * HALF] = pltpu.roll(main[q, WIDE:], LANES // 2, 1)
                for first_row, count, x in ((0, per, main.at[q]), (per, shard_rows - per, tail.at[q])):
                    shifts = [x[dc : dc + wide] for dc in range(3)]
                    for r in range(count):
                        y = jnp.zeros((wide, LANES), jnp.float32)
                        for dc in (2, 1, 0):
                            turn = (dc - r) * clat % LANES
                            moved = pltpu.roll(shifts[dc], turn, 1) if turn else shifts[dc]
                            y = jnp.where(at_lane < (dc + 1) * clat, moved, y)
                        start = row_at(1 + q * shard_rows + first_row + r)
                        rowtap[start : start + wide] = y

            for w in range(aw):
                v = [rowtap[pl.ds(row_at(k) + w, hh, stride=pitch), :] for k in range(4)]
                turned = [pltpu.roll(v[k], GAP, 1) for k in (1, 2)]
                low = jnp.concatenate([v[0] + turned[0], v[1] + turned[1]])
                z_ref[f, w, :, :LANES] = low.astype(jnp.bfloat16)
                z_ref[f, w, :, LANES:] = jnp.concatenate(v[2:]).astype(jnp.bfloat16)

    each_send(finish)


def decode_kernel(
    sizes, clip, z_ref, w1_ref, g1_ref, u_ref, g2_ref, hw_ref, out_ref,
    v_ref, v3_ref, va_ref, vb_ref, r_ref, firstb, fscr, ya_ref, yb_ref, outw, head_ref,
):
    tiles, strips, hl, clat, shard_rows = sizes
    ch = g1_ref.shape[-1]
    patch = hw_ref.shape[0] // 3
    half = patch // 2
    aw = WS + 3
    ow = WS + 1
    hh = hl // 2
    lanes = WS * half
    rotated = (lax.axis_index("tile") + tiles - (strips // 2 - 1)) % tiles
    strip = rotated % strips
    block = rotated // strips

    def clip_of(i):
        at = block * TF - 2 * TF + i
        return jnp.where(at < 0, -1, clip[jnp.maximum(at, 0)])

    scal = [clip_of(i) for i in range(3 * TF)]
    g1 = g1_ref[...].reshape(1, ch)
    g2 = g2_ref[...].reshape(1, ch)

    same12 = scal[3] == scal[4]
    same23 = scal[4] == scal[5]
    same02 = scal[2] == scal[4]
    def first_dot(f, keeps, at):
        count = len(keeps)
        taps = [z_ref[f + 3 - count + k].reshape(aw * hl, -1) for k in range(count)]
        taps = [x if keep is None else jnp.where(keep, x, 0) for x, keep in zip(taps, keeps)]
        fscr[at] = jnp.dot(
            jnp.concatenate(taps, axis=-1), w1_ref[3 - count :].reshape(-1, ch),
            preferred_element_type=jnp.float32,
        ).reshape(aw, hl, ch)

    def first_norm(f, w, at, inside):
        rounded = fscr[at, w].astype(jnp.bfloat16)
        if not isinstance(f, int):
            firstb[jnp.maximum(f - 2, 0), w] = rounded
        elif f >= 2:
            firstb[f - 2, w] = rounded
        value = norm_act(rounded.astype(jnp.float32), g1)
        if inside is not None:
            value = value * inside.astype(jnp.float32)
        even, odd = value[:hh], value[hh:]
        r_ref[f, w, 0] = row_shift(odd, 1) - odd
        r_ref[f, w, 1] = even + odd
        r_ref[f, w, 2] = odd - even
        r_ref[f, w, 3] = even - row_shift(even, -1)

    def first(f, *keeps):
        first_dot(f, keeps, f % 2)
        for w in range(aw):
            first_norm(f, w, f % 2, strip > 0 if w < 2 else strip < strips - 1 if w == aw - 1 else None)

    def expand(f, i, dst):
        for c in range(0, PAIRS, 2):
            d = [r_ref[f, 2 * c + k, i] for k in range(min(6, aw - 2 * c))]
            cells = [[d[0] - d[2], d[1] + d[2], d[2] - d[1], d[1] - d[3] if len(d) > 3 else d[1]]]
            if c + 1 < PAIRS:
                cells.append([d[2] - d[4], d[3] + d[4], d[4] - d[3], d[3] - d[5]])
            else:
                cells.append([jnp.zeros((8, ch), jnp.float32)] * 4)
            for j in range(4):
                both = jnp.concatenate([cell[j] for cell in cells])
                dst[j, c * hh : c * hh + both.shape[0]] = both.astype(jnp.bfloat16)

    def product(sides, weights):
        return jnp.dot(
            jnp.concatenate(sides, axis=-1), jnp.concatenate(weights, axis=0),
            preferred_element_type=jnp.float32,
        )

    def product_both(sides, comp):
        w0, w1, w2 = [u_ref[comp, dt] for dt in range(3)]
        return product(
            sides, [jnp.concatenate([w1, w0], axis=-1), jnp.concatenate([w2, w1], axis=-1)]
        )

    def put(y, i, sums):
        y[i, 0], y[i, 1] = pair_outputs(sums)

    def put_more(y, i, sums):
        front, back = pair_outputs(sums)
        y[i, 0] += front
        y[i, 1] += back

    rows = lax.broadcasted_iota(jnp.int32, (3 * patch, 6 * lanes), 0)
    cols = lax.broadcasted_iota(jnp.int32, (3 * patch, 6 * lanes), 1)
    odd = cols // (3 * lanes)
    colour = (cols // lanes) % 3
    want = colour * patch + (cols % lanes + half * odd) % patch
    spread = (rows == want).astype(jnp.bfloat16)
    head_ref[...] = lax.dot_general(
        hw_ref[...], spread, (((0,), (0,)), ((), ())), preferred_element_type=jnp.float32
    ).astype(jnp.bfloat16)
    lane = lax.broadcasted_iota(jnp.int32, (hl, lanes), 1)

    def outward(fo, y, cell, side):
        part = pl.ds(pl.multiple_of(cell * hh, 8), hh)
        added = jnp.concatenate(pair_outputs([y[i, side, part] for i in range(4)]))
        value = norm_act(firstb[fo, 2 * cell + side + 1].astype(jnp.float32) + added, g2)
        if side == 0:
            value = value * jnp.logical_or(cell > 0, strip > 0).astype(jnp.float32)
        outw[side, cell] = value.astype(jnp.bfloat16)

    def picture(fo):
        p_odd = jnp.dot(
            outw[0].reshape(-1, ch), head_ref[:, 3 * lanes :], preferred_element_type=jnp.float32
        )
        p_even = jnp.dot(
            outw[1, : WS // 2].reshape(-1, ch), head_ref[:, : 3 * lanes],
            preferred_element_type=jnp.float32,
        )
        for k in range(3):
            front = jnp.zeros((hl, lanes), jnp.float32)
            back = jnp.zeros((hl, lanes), jnp.float32)
            for i in range(WS // 2):
                piece = p_even[i * hl : (i + 1) * hl, k * lanes : (k + 1) * lanes]
                front = jnp.where(lane // patch == i, piece, front)
            for i in range(WS // 2 + 1):
                piece = p_odd[i * hl : (i + 1) * hl, k * lanes : (k + 1) * lanes]
                back = jnp.where((lane + half) // patch == i, piece, back)
            out_ref[fo, k, pl.ds(0, hh, stride=2), :] = (front + back)[:hh]
            out_ref[fo, k, pl.ds(1, hh, stride=2), :] = (front + back)[hh:]

    late = jnp.logical_not(same02)
    early = jnp.logical_and(jnp.logical_and(same02, jnp.logical_not(same23)), scal[1] != scal[2])

    def all_outward(fo, y):
        for w in range(ow):
            outward(fo, y, w // 2, w % 2)
        picture(fo)

    def halves(body):
        @pl.loop(0, 2)
        def _(pair):
            body(2 * pair, va_ref, vb_ref)
            body(2 * pair + 1, vb_ref, va_ref)

    def quarters_of(body):
        for pair in range(2):
            body(2 * pair, va_ref, vb_ref)
            body(2 * pair + 1, vb_ref, va_ref)

    @pl.when(late)
    def _():
        @pl.when(same12)
        def _():
            first(1, None)

        @pl.when(jnp.logical_not(same12))
        def _():
            r_ref[1] = jnp.zeros(r_ref.shape[1:], jnp.float32)

        first(2, same12, None)
        expand(1, 0, va_ref.at[0])
        expand(2, 0, va_ref.at[1])
        first(3, scal[3] == scal[5], same23, None)
        use_last = same23.astype(jnp.float32)

        def both(i, now, later):
            after = min(i + 1, 3)
            sums = []
            for j in range(4):
                sums.append(product_both([now[0, j], now[1, j]], 4 * i + j))
                if j in (1, 2):
                    expand(j, after, later.at[j - 1])
                if j == 3:
                    expand(3, i, v3_ref.at[pl.ds(4 * i, 4)])
            put(ya_ref, i, [x[:, :ch] for x in sums])
            put(yb_ref, i, [use_last * x[:, ch:] for x in sums])

        def last(i, now, later):
            sums = [product([v3_ref[4 * i + j]], [u_ref[4 * i + j, 2]]) for j in range(4)]
            for k in range(4):
                outward(0, ya_ref, 2 * i + k // 2, k % 2)
            put_more(yb_ref, i, sums)

        quarters_of(both)
        quarters_of(last)
        outward(0, ya_ref, WS // 2, 0)
        picture(0)

    @pl.when(early)
    def _():
        first(3, None)
        first(2, None, None, None)
        for i in range(4):
            expand(3, i, v3_ref.at[pl.ds(4 * i, 4)])
        first(1, None, None)
        first(0, None)

        def alone(i, now, later):
            sums = []
            for j in range(4):
                sums.append(product([v3_ref[4 * i + j]], [u_ref[4 * i + j, 2]]))
                if j < 3:
                    expand(j, i, v_ref.at[j, pl.ds(4 * i, 4)])
            put(ya_ref, i, sums)

        def three(i, now, later):
            sums = [
                product(
                    [v_ref[f, 4 * i + j] for f in range(3)], [u_ref[4 * i + j, dt] for dt in range(3)]
                )
                for j in range(4)
            ]
            for k in range(4):
                outward(1, ya_ref, 2 * i + k // 2, k % 2)
            put(yb_ref, i, sums)

        quarters_of(alone)
        quarters_of(three)
        outward(1, ya_ref, WS // 2, 0)
        picture(1)

    @pl.when(jnp.logical_not(jnp.logical_or(late, early)))
    def _():
        ya_ref[...] = jnp.zeros_like(ya_ref)
        yb_ref[...] = jnp.zeros_like(yb_ref)

        @pl.loop(0, TF + 2)
        def _(f):
            ids = [clip_of(f + dt) for dt in range(3)]
            first_dot(f, [ids[0] == ids[2], ids[1] == ids[2], None], 0)

            @pl.loop(0, aw)
            def _(w):
                first_norm(f, w, 0, ((strip > 0) | (w >= 2)) & ((strip < strips - 1) | (w < aw - 1)))

            @pl.loop(0, 4)
            def _(i):
                expand(f, i, v3_ref.at[pl.ds(4 * i, 4)])

            for fo, y in enumerate((ya_ref, yb_ref)):

                @pl.when(jnp.logical_and(jnp.logical_and(f >= fo, f <= fo + 2), ids[2] == scal[4 + fo]))
                def _(fo=fo, y=y):
                    @pl.loop(0, 4)
                    def _(i):
                        @pl.loop(0, 4)
                        def _(j):
                            one = product([v3_ref[4 * i + j]], [u_ref[4 * i + j, f - fo]])
                            y[i, 0] += jnp.where(j == 0, 1.0, jnp.where(j == 3, 0.0, 0.5)) * one
                            y[i, 1] += jnp.where(j == 0, 0.0, jnp.where(j == 3, -1.0, 1.5 - j)) * one

        all_outward(0, ya_ref)

    all_outward(jnp.where(early, 0, 1), yb_ref)


def decode_call(sizes, patch, ch, operands):
    tiles, strips, hl, clat, shard_rows = sizes
    aw = WS + 3
    half = patch // 2
    mrows = -(-PAIRS * (hl // 2) // 16) * 16
    vm = pl.BlockSpec(memory_space=pltpu.VMEM)
    return pl.pallas_call(
        functools.partial(decode_kernel, sizes),
        out_shape=jax.ShapeDtypeStruct((TF, 3, hl, WS * half), jnp.float32),
        in_specs=[pl.BlockSpec(memory_space=pltpu.SMEM)] + [vm] * 6,
        out_specs=vm,
        scratch_shapes=[
            pltpu.VMEM((TF + 1, 16, mrows, ch), jnp.bfloat16),
            pltpu.VMEM((16, mrows, ch), jnp.bfloat16),
            pltpu.VMEM((2, 4, mrows, ch), jnp.bfloat16),
            pltpu.VMEM((2, 4, mrows, ch), jnp.bfloat16),
            pltpu.VMEM((TF + 2, aw, 4, hl // 2, ch), jnp.float32),
            pltpu.VMEM((TF, aw, hl, ch), jnp.bfloat16),
            pltpu.VMEM((2, aw, hl, ch), jnp.float32),
            pltpu.VMEM((4, 2, mrows, ch), jnp.float32),
            pltpu.VMEM((4, 2, mrows, ch), jnp.float32),
            pltpu.VMEM((2, WS // 2 + 1, hl, ch), jnp.bfloat16),
            pltpu.VMEM((ch, 6 * WS * half), jnp.bfloat16),
        ],
        compiler_params=pltpu.CompilerParams(vmem_limit_bytes=40 * 1024 * 1024),
    )(*operands)


def per_device(latents, clip_index, first_conv, first_gain, middle_conv, head_gain, head_weight):
    tiles = lax.axis_size("tile")
    shard_rows, clat, wl = latents.shape
    ch = first_gain.shape[0]
    frames = clip_index.shape[0]
    hl = tiles * shard_rows // frames
    strips = wl // WS
    quarters = tiles // frames
    slots = 3 * TF * quarters
    vm = pl.BlockSpec(memory_space=pltpu.VMEM)
    fields, sums, first_taps = pl.pallas_call(
        functools.partial(exchange_kernel, (tiles, strips, frames, shard_rows)),
        out_shape=[
            pltpu.VMEM((3 * TF, WS + 3, hl, 2 * LANES), jnp.bfloat16),
            pltpu.VMEM((16, 3, ch, ch), jnp.bfloat16),
            pltpu.VMEM((3, 2 * LANES, ch), jnp.bfloat16),
        ],
        in_specs=[pl.BlockSpec(memory_space=pl.ANY)] * 3,
        out_specs=[vm] * 3,
        scratch_shapes=[
            pltpu.VMEM((slots, WIDE + HALF, LANES), jnp.bfloat16),
            pltpu.VMEM((shard_rows * clat, wl), jnp.bfloat16),
            pltpu.VMEM((8 + wl + WS, LANES), jnp.float32),
            pltpu.VMEM((8 + wl + WS, LANES), jnp.float32),
            pltpu.VMEM((strips, WIDE + HALF, LANES), jnp.float32),
            pltpu.VMEM((strips, WIDE + HALF, LANES), jnp.bfloat16),
            pltpu.VMEM((3, 3, 3, ch, ch), jnp.bfloat16),
            pltpu.VMEM((quarters, WIDE + HALF, LANES), jnp.float32),
            pltpu.VMEM((quarters, WIDE + HALF, LANES), jnp.float32),
            pltpu.VMEM((2 * (-(-(hl // 2 + 1) * (-(-WIDE // 8) * 8 + 1) // 8) * 8), LANES), jnp.float32),
            pltpu.SemaphoreType.DMA((3 * strips,)),
            pltpu.SemaphoreType.DMA((slots,)),
            pltpu.SemaphoreType.DMA,
            pltpu.SemaphoreType.DMA,
            pltpu.SemaphoreType.DMA((3,)),
            pltpu.SemaphoreType.DMA((9,)),
        ],
        compiler_params=pltpu.CompilerParams(
            collective_id=0, has_side_effects=True, vmem_limit_bytes=40 * 1024 * 1024
        ),
    )(*[
        pltpu.with_memory_space_constraint(x, pltpu.HBM)
        for x in (latents.reshape(shard_rows * clat, wl), middle_conv, first_conv.reshape(3, 9 * clat, ch))
    ])
    fields, sums, first_taps = [
        pltpu.with_memory_space_constraint(x, pltpu.VMEM) for x in (fields, sums, first_taps)
    ]
    out = decode_call(
        (tiles, strips, hl, clat, shard_rows), head_weight.shape[1] // 3, ch,
        (clip_index, fields, first_taps, first_gain, sums, head_gain, head_weight.T),
    )
    return out[None]


def solution(mesh):
    placed = (P(("group", "tile"), None, None), P("group"), P(), P(), P(), P(), P())
    return jax.shard_map(
        per_device,
        mesh=mesh,
        in_specs=placed,
        out_specs=P(("group", "tile"), None, None, None, None),
        check_vma=False,
    )
```
